128 devices in a mesh: expert: 8 (over z, core), fsdp: 16 (over y, x).
Axes of the slice: x: 4, y: 4, z: 4, core: 2. Of those that a mesh axis runs over, the one named last changes fastest.
Arguments:
- tokens: bfloat16 [32768, 2048], P(('expert', 'fsdp')), may hold values from -6 to 6
- expert_ids: int32 [32768, 6], P(('expert', 'fsdp')), may hold values from 0 to 63, as said below
- gate_vals: bfloat16 [32768, 6], P(('expert', 'fsdp')), may hold values from 0.099609375 to 1
- w_gate: bfloat16 [8, 2048, 1408], P('expert', 'fsdp'), may hold values from -0.125 to 0.125
- w_up: bfloat16 [8, 2048, 1408], P('expert', 'fsdp'), may hold values from -0.125 to 0.125
- w_down: bfloat16 [8, 2048, 1408], P('expert', 'fsdp'), may hold values from -0.15625 to 0.15625
- cotangent: bfloat16 [32768, 2048], P(('expert', 'fsdp')), may hold values from -6 to 6
Outputs:
- output: bfloat16 [32768, 2048], P(('expert', 'fsdp'))
- grad_tokens: bfloat16 [32768, 2048], P(('expert', 'fsdp'))
- grad_gates: float32 [32768, 6], P(('expert', 'fsdp'))
- grad_w_gate: float32 [8, 2048, 1408], P('expert', 'fsdp')
- grad_w_up: float32 [8, 2048, 1408], P('expert', 'fsdp')
- grad_w_down: float32 [8, 2048, 1408], P('expert', 'fsdp')
The draws below stay inside these ranges and needn't reach their ends.
Inputs may be any that keep to these rules, and one draw needn't show every extreme that they name: `expert_ids`: each row names 6 different experts. Among the tokens of one device at most 48 name any one expert whose number modulo 8 is below 1. On every device some such expert is named by exactly 48 of its tokens, and for every column one such expert is named by exactly 48 tokens of every device of that column.
All inputs are finite; a program needn't handle non-finite values.
Results may differ from the reference program's by a relative error of at most 0.013.
Values may be sent and summed in bfloat16 or wider, within the bound.
No kernel may reach another device: no remote copies, remote signals or barrier semaphores. Data moves between devices by JAX's collectives and lax.ppermute only.
A program may use at most 128 MiB of HBM per device.

```python
import jax
import jax.numpy as jnp
from jax import lax

D = 2048
FF = 1408
EXPERTS = 64
TOP = 6
TOK_DEV = 256
WAVE = 1
GROUPS = 8
COLUMNS = 16
PER_INDEX = 8
WINDOW = 8
MOST = 48
TOKENS = 32768


def block_routes(key, block):
    column_index = block % COLUMNS
    hot_pick = jax.random.randint(jax.random.fold_in(key, 7), (COLUMNS,), 0, WINDOW)[column_index]
    block_key = jax.random.fold_in(key, block + 11)
    key_shift, key_perm, key_score, key_order = jax.random.split(block_key, 4)
    shifts = jax.random.randint(key_shift, (WINDOW,), 0, 3)
    levels = jnp.array([MOST, MOST // 2, MOST // 4], jnp.int32)
    counts = levels[shifts]
    counts = jnp.where(jnp.arange(WINDOW) == hot_pick, MOST, counts).astype(jnp.int32)
    starts = jnp.cumsum(counts) - counts
    position = jnp.arange(TOK_DEV, dtype=jnp.int32)
    covered = (position[:, None] - starts[None, :]) % TOK_DEV < counts[None, :]
    shuffle = jax.random.permutation(key_perm, TOK_DEV)
    token_cover = covered[shuffle]
    window_ids = jnp.arange(WINDOW, dtype=jnp.int32)
    window_expert = window_ids // WAVE * PER_INDEX + window_ids % WAVE
    cover_full = jnp.zeros((TOK_DEV, EXPERTS), jnp.bool_).at[:, window_expert].set(token_cover)
    expert_range = jnp.arange(EXPERTS, dtype=jnp.int32)
    in_window = expert_range % PER_INDEX < WAVE
    base = jax.random.randint(key_score, (TOK_DEV, EXPERTS), 0, 2 ** 16) * EXPERTS + expert_range[None, :]
    chosen_score = jnp.where(cover_full, 2 ** 30 + expert_range[None, :], -1 - expert_range[None, :])
    score = jnp.where(in_window[None, :], chosen_score, base)
    unused, picks = lax.top_k(score, TOP)
    order_keys = jax.random.randint(key_order, (TOK_DEV, TOP), 0, 2 ** 16) * TOP + jnp.arange(TOP, dtype=jnp.int32)[None, :]
    slot_order = jnp.argsort(order_keys, axis=1)
    return jnp.take_along_axis(picks, slot_order, axis=1).astype(jnp.int32)


def draw_expert_ids(key, part):
    blocks = jnp.arange(GROUPS * COLUMNS, dtype=jnp.int32)
    routed = jax.vmap(lambda block: block_routes(key, block))(blocks)
    return routed.reshape(TOKENS, TOP).astype(jnp.int32)


def block_scale(rng, shape, pieces, least, largest):
    gain, own = 1.0, jax.random.fold_in(rng, 6)
    for dim, blocks in pieces:
        heights = jnp.exp(jax.random.uniform(jax.random.fold_in(own, dim), (blocks,), jnp.float32, least / len(pieces), largest / len(pieces)))
        gain = gain * jnp.repeat(heights, shape[dim] // blocks).reshape([-1 if axis == dim else 1 for axis in range(len(shape))])
    return gain


def normal_values(stream_key, dims, spread, reach, cuts=(), kind=jnp.bfloat16):
    factor_of = block_scale(stream_key, dims, cuts, -0.22, 0.18) if cuts else 1.0
    values = jax.random.normal(stream_key, dims, jnp.float32) * spread * factor_of
    return jnp.minimum(jnp.maximum(values, -reach), reach).astype(kind)


def setup_inputs(seed: int = 0) -> dict:
    arg_keys = jax.random.split(jax.random.key(seed), 8)
    tokens = normal_values(arg_keys[0], (TOKENS, D), 1.0, 6.0, ((0, 128),))
    expert_ids = draw_expert_ids(jax.random.fold_in(arg_keys[7], 71), 0)
    gate_vals = jnp.clip(0.099609375 + 0.9003906 * jax.random.uniform(arg_keys[2], (TOKENS, TOP), jnp.float32) ** block_scale(arg_keys[2], (TOKENS, TOP), ((0, 128),), -0.2, 0.2), 0.099609375, 1.0).astype(jnp.bfloat16)
    w_gate = normal_values(arg_keys[3], (WINDOW, D, FF), D ** -0.5, 0.125, ((0, 8), (1, 16)))
    w_up = normal_values(arg_keys[4], (WINDOW, D, FF), D ** -0.5, 0.125, ((0, 8), (1, 16)))
    w_down = normal_values(arg_keys[5], (WINDOW, D, FF), FF ** -0.5, 0.15625, ((0, 8), (1, 16)))
    cotangent = normal_values(arg_keys[6], (TOKENS, D), 1.0, 6.0, ((0, 128),))
    return {"tokens": tokens, "expert_ids": expert_ids, "gate_vals": gate_vals, "w_gate": w_gate, "w_up": w_up, "w_down": w_down, "cotangent": cotangent}


def reference(tokens, expert_ids, gate_vals, w_gate, w_up, w_down, cotangent):
    slot_total = TOKENS * TOP
    model_width = tokens.shape[1]
    flat_ids = expert_ids.reshape(-1).astype(jnp.int32)
    local_index = flat_ids % PER_INDEX
    is_live = local_index < WAVE
    window_slot = jnp.where(is_live, (flat_ids // PER_INDEX) * WAVE + local_index, WINDOW).astype(jnp.int32)
    slot_ids = jnp.arange(slot_total, dtype=jnp.int32)
    column = ((slot_ids // TOP) // TOK_DEV) % COLUMNS
    zero_row = jnp.zeros((1, model_width), tokens.dtype)
    tokens_pad = jnp.concatenate([tokens, zero_row], axis=0)
    cot_pad = jnp.concatenate([cotangent, zero_row], axis=0)
    gate_pad = jnp.concatenate([gate_vals.reshape(-1), jnp.zeros((1,), gate_vals.dtype)], axis=0)
    capacity = GROUPS * MOST

    def pair_step(running, column_index, expert):
        out_acc, grad_acc, gate_acc, sum_gate, sum_up, sum_down = running
        chosen = (window_slot == expert) & (column == column_index)
        picked = jnp.nonzero(chosen, size=capacity, fill_value=slot_total)[0].astype(jnp.int32)
        token_at = (picked // TOP).astype(jnp.int32)
        row_data = tokens_pad[token_at]
        cot_rows = cot_pad[token_at]
        gate_rows = gate_pad[picked].astype(jnp.float32)
        weight_gate = w_gate[expert]
        weight_up = w_up[expert]
        weight_down = w_down[expert]
        gate_pre = jnp.dot(row_data, weight_gate, preferred_element_type=jnp.float32)
        up_pre = jnp.dot(row_data, weight_up, preferred_element_type=jnp.float32)
        sigmoid_g = jax.nn.sigmoid(gate_pre)
        hidden = (gate_pre * sigmoid_g * up_pre).astype(jnp.bfloat16)
        expert_out = jnp.dot(hidden, weight_down.T, preferred_element_type=jnp.float32).astype(jnp.bfloat16)
        out_f = expert_out.astype(jnp.float32)
        out_acc = out_acc.at[token_at].add(gate_rows[:, None] * out_f, mode="drop")
        gate_acc = gate_acc.at[picked].add(jnp.sum(cot_rows.astype(jnp.float32) * out_f, axis=1), mode="drop")
        out_grad = (gate_rows[:, None] * cot_rows.astype(jnp.float32)).astype(jnp.bfloat16)
        hidden_grad = jnp.dot(out_grad, weight_down, preferred_element_type=jnp.float32)
        gate_grad = (hidden_grad * up_pre * sigmoid_g * (1.0 + gate_pre * (1.0 - sigmoid_g))).astype(jnp.bfloat16)
        up_grad = (hidden_grad * gate_pre * sigmoid_g).astype(jnp.bfloat16)
        slot_grad = (jnp.dot(gate_grad, weight_gate.T, preferred_element_type=jnp.float32)
                     + jnp.dot(up_grad, weight_up.T, preferred_element_type=jnp.float32)).astype(jnp.bfloat16)
        grad_acc = grad_acc.at[token_at].add(slot_grad.astype(jnp.float32), mode="drop")
        part_gate = jnp.dot(row_data.T, gate_grad, preferred_element_type=jnp.float32).astype(jnp.bfloat16)
        part_up = jnp.dot(row_data.T, up_grad, preferred_element_type=jnp.float32).astype(jnp.bfloat16)
        part_down = jnp.dot(out_grad.T, hidden, preferred_element_type=jnp.float32).astype(jnp.bfloat16)
        sum_gate = sum_gate + part_gate.astype(jnp.float32)
        sum_up = sum_up + part_up.astype(jnp.float32)
        sum_down = sum_down + part_down.astype(jnp.float32)
        return (out_acc, grad_acc, gate_acc, sum_gate, sum_up, sum_down)

    def expert_step(running, expert):
        zeros_w = jnp.zeros((model_width, FF), jnp.float32)
        inside = (running[0], running[1], running[2], zeros_w, zeros_w, zeros_w)

        def column_step(state, column_index):
            return pair_step(state, column_index, expert), None

        inside, unused = lax.scan(column_step, inside, jnp.arange(COLUMNS, dtype=jnp.int32))
        return (inside[0], inside[1], inside[2]), (inside[3], inside[4], inside[5])

    initial = (jnp.zeros((TOKENS, model_width), jnp.float32),
               jnp.zeros((TOKENS, model_width), jnp.float32),
               jnp.zeros((slot_total,), jnp.float32))
    finished, weight_grads = lax.scan(expert_step, initial, jnp.arange(WINDOW, dtype=jnp.int32))
    output = finished[0].astype(jnp.bfloat16)
    grad_tokens = finished[1].astype(jnp.bfloat16)
    grad_gates = finished[2].reshape(TOKENS, TOP)
    return output, grad_tokens, grad_gates, weight_grads[0], weight_grads[1], weight_grads[2]
```

```python
import functools

import jax
import jax.numpy as jnp
from jax import lax
from jax.experimental import pallas as pl
from jax.experimental.pallas import tpu as pltpu
from jax.sharding import PartitionSpec as P

TOP = 6
MOST = 48
OWNED = 8
LANE = 128
AXES = ("expert", "fsdp")
F32 = jnp.float32
BF16 = jnp.bfloat16


def pairs_of(move):
    pairs = []
    for source in range(128):
        z, core, y, x = source // 32, source // 16 % 2, source // 4 % 4, source % 4
        core, y, x = move(core, y, x)
        pairs.append((source, (z * 2 + core) * 16 + y % 4 * 4 + x))
    return pairs


TO_CORE = pairs_of(lambda core, y, x: (1 - core, y, x))
TO_MIRROR = pairs_of(lambda core, y, x: (core, y, 3 - x))
TO_SIDE = pairs_of(lambda core, y, x: (core, y, x ^ 1))
TO_UP = pairs_of(lambda core, y, x: (core, y + 1, x))
TO_DOWN = pairs_of(lambda core, y, x: (core, y - 1, x))
Z_GROUPS = [[0, 2, 4, 6], [1, 3, 5, 7]]


def send(value, pairs):
    return lax.ppermute(value, AXES, pairs)


def routes(ids, half, own):
    tok_count = ids.shape[1]
    side = half if own else 1 - half
    live = []
    for z in range(4):
        wanted = OWNED * (2 * z + side)
        live.append(jnp.sum(jnp.where(ids == wanted, 1.0, 0.0), axis=0, keepdims=True))
    live = jnp.concatenate(live + [jnp.zeros((4, tok_count), F32)], axis=0)
    before = lax.broadcasted_iota(jnp.int32, (tok_count, tok_count), 0)
    after = lax.broadcasted_iota(jnp.int32, (tok_count, tok_count), 1)
    earlier = jnp.where(before < after, 1.0, 0.0).astype(BF16)
    rank = jnp.dot(live.astype(BF16), earlier, preferred_element_type=F32)
    row = lax.broadcasted_iota(jnp.int32, (MOST, tok_count), 0).astype(F32)
    chosen = []
    for z in range(4):
        here = jnp.where(row == rank[z : z + 1], 1.0, 0.0) * live[z : z + 1]
        chosen.append(here)
    return chosen


def gates_of(ids, gates, half, own):
    side = half if own else 1 - half
    return [
        jnp.sum(jnp.where(ids == OWNED * (2 * z + side), gates, 0.0), axis=0, keepdims=True)
        for z in range(4)
    ]


def dispatch_kernel(place, ids_ref, gates_ref, tok_ref, cot_ref, *outs):
    y, half = place[0], place[1]
    ids = ids_ref[...]
    gates = gates_ref[...].astype(F32)
    width = tok_ref.shape[1] // 8
    for own in (True, False):
        rows_ref, grad_ref = (outs[0], outs[2]) if own else (outs[1], outs[3])
        chosen = routes(ids, half, own)
        gate = gates_of(ids, gates, half, own)
        weight = jnp.concatenate(
            [jnp.sum(s * g, axis=1, keepdims=True) for s, g in zip(chosen, gate)], axis=0
        )
        select = jnp.concatenate(chosen, axis=0).astype(BF16)
        side = half if own else 1 - half
        for kind in range(2):
            for step in range(4):
                block = lax.rem(y + step, 4) * 2 + (side if kind == 0 else 1 - side)
                read = pl.ds(pl.multiple_of(block * width, width), width)
                put = slice((kind * 4 + step) * width, (kind * 4 + step + 1) * width)
                rows = jnp.dot(select, tok_ref[:, read], preferred_element_type=F32)
                rows_ref[:, put] = rows.astype(BF16)
                cots = jnp.dot(select, cot_ref[:, read], preferred_element_type=F32)
                grad_ref[:, put] = (weight * cots).astype(BF16)


def dispatch(place, ids, gates, tokens, cotangent):
    width = tokens.shape[1]
    rows = jax.ShapeDtypeStruct((4 * MOST, width), BF16)
    whole = pl.BlockSpec(memory_space=pltpu.VMEM)
    return pl.pallas_call(
        dispatch_kernel,
        out_shape=(rows,) * 4,
        in_specs=[pl.BlockSpec(memory_space=pltpu.SMEM)] + [whole] * 4,
        out_specs=(whole,) * 4,
        compiler_params=pltpu.CompilerParams(vmem_limit_bytes=48 << 20),
        cost_estimate=pl.CostEstimate(
            flops=1_000_000_000, bytes_accessed=6_000_000, transcendentals=0
        ),
        name="dispatch",
    )(place, ids, gates, tokens, cotangent)


TURNED = (((0,), (0,)), ((), ()))


def combine_kernel(
    place, ids_ref, gates_ref, cot_ref, own_ref, oth_ref, gown_ref, goth_ref, out_ref, gtok_ref, gg_ref
):
    y, half = place[0], place[1]
    ids = ids_ref[...]
    gates = gates_ref[...].astype(F32)
    width = cot_ref.shape[1] // 8
    picked, weighted, chosen_of = [], [], []
    for own in (True, False):
        chosen = routes(ids, half, own)
        gate = gates_of(ids, gates, half, own)
        picked.append(jnp.concatenate(chosen, axis=0).astype(BF16))
        weighted.append(
            jnp.concatenate([s * g for s, g in zip(chosen, gate)], axis=0).astype(BF16)
        )
        chosen_of.append(chosen)
    totals = [jnp.zeros((4 * MOST, 1), F32) for _ in range(2)]
    for step in range(4):
        for kind in range(2):
            block = lax.rem(y + step, 4) * 2 + (half if kind == 0 else 1 - half)
            at = pl.ds(pl.multiple_of(block * width, width), width)
            mine = slice((kind * 4 + step) * width, (kind * 4 + step + 1) * width)
            other = slice(((1 - kind) * 4 + step) * width, ((1 - kind) * 4 + step + 1) * width)
            cot = cot_ref[:, at]
            outs = (own_ref[:, mine], oth_ref[:, other])
            grads = (gown_ref[:, mine], goth_ref[:, other])
            out_ref[:, at] = sum(
                lax.dot_general(w, o, TURNED, preferred_element_type=F32)
                for w, o in zip(weighted, outs)
            ).astype(BF16)
            gtok_ref[:, at] = sum(
                lax.dot_general(s, g, TURNED, preferred_element_type=F32)
                for s, g in zip(picked, grads)
            ).astype(BF16)
            for i in range(2):
                cots = jnp.dot(picked[i], cot, preferred_element_type=F32)
                totals[i] += jnp.sum(cots * outs[i].astype(F32), axis=1, keepdims=True)
    result = jnp.zeros(ids.shape, F32)
    for i, own in enumerate((True, False)):
        side = half if own else 1 - half
        for z in range(4):
            per_slot = totals[i][z * MOST : (z + 1) * MOST]
            per_token = jnp.sum(chosen_of[i][z] * per_slot, axis=0, keepdims=True)
            result += jnp.where(ids == OWNED * (2 * z + side), per_token, 0.0)
    gg_ref[...] = result


def combine(place, ids, gates, cotangent, own, oth, gown, goth):
    shape = jax.ShapeDtypeStruct(cotangent.shape, BF16)
    whole = pl.BlockSpec(memory_space=pltpu.VMEM)
    return pl.pallas_call(
        combine_kernel,
        out_shape=(shape, shape, jax.ShapeDtypeStruct(ids.shape, F32)),
        in_specs=[pl.BlockSpec(memory_space=pltpu.SMEM)] + [whole] * 7,
        out_specs=(whole,) * 3,
        compiler_params=pltpu.CompilerParams(vmem_limit_bytes=48 << 20),
        cost_estimate=pl.CostEstimate(
            flops=2_000_000_000, bytes_accessed=8_000_000, transcendentals=0
        ),
        name="combine",
    )(place, ids, gates, cotangent, own, oth, gown, goth)


def half_width(width):
    return -(-width // (2 * LANE)) * LANE


def gather_weights(weights, core, side, low):
    width = weights.shape[2]
    part = half_width(width)
    left = weights[:, :, :part]
    blank = jnp.zeros(weights.shape[:2] + (2 * part - width,), weights.dtype)
    right = jnp.concatenate([blank, weights[:, :, part:]], axis=2)
    keep = jnp.where(core == 0, left, right)
    give = jnp.where(core == 0, right, left)
    got = send(give, TO_CORE)
    own = jnp.where(core == side, keep, got)
    away = jnp.where(core == side, got, keep)
    beside = send(own, TO_SIDE)
    mirror = send(away, TO_MIRROR)
    block = jnp.where(
        low == 0,
        jnp.concatenate([own, beside], axis=1),
        jnp.concatenate([beside, own], axis=1),
    )
    block3 = send(block, TO_UP)
    block1 = send(block, TO_DOWN)
    mirror3 = send(mirror, TO_UP)
    mirror1 = send(mirror, TO_DOWN)
    block2 = send(block3, TO_UP)
    mirror2 = send(mirror1, TO_DOWN)
    mine = jnp.stack([mirror, mirror1, mirror2, mirror3], axis=1)
    theirs = send(mine, TO_SIDE)
    mirrors = jnp.where(
        low == 1,
        jnp.concatenate([mine, theirs], axis=2),
        jnp.concatenate([theirs, mine], axis=2),
    )
    n, rows = weights.shape[:2]
    return jnp.concatenate(
        [block, block1, block2, block3, mirrors.reshape(n, 8 * rows, part)], axis=1
    )


def add(*terms):
    return sum(t.astype(F32) for t in terms).astype(BF16)


def scatter_sums(terms, width, core, side, low):
    n, depth, part = terms.shape
    rows = depth // 16
    block = terms[:, : depth // 2].reshape(n, 4, 2 * rows, part)
    mirrors = terms[:, depth // 2 :].reshape(n, 4, 2, rows, part)
    keep = jnp.where(low == 1, mirrors[:, :, 0], mirrors[:, :, 1])
    give = jnp.where(low == 1, mirrors[:, :, 1], mirrors[:, :, 0])
    far = send(block[:, 2], TO_UP)
    back = send(block[:, 3], TO_DOWN)
    got = send(give, TO_SIDE)
    near = send(add(far, block[:, 1]), TO_UP)
    kept = add(keep, got)
    far_m = send(kept[:, 2], TO_DOWN)
    back_m = send(kept[:, 1], TO_UP)
    two = add(block[:, 0], back, near)
    near_m = send(add(far_m, kept[:, 3]), TO_DOWN)
    stay = jnp.where(low == 0, two[:, :rows], two[:, rows:])
    leave = jnp.where(low == 0, two[:, rows:], two[:, :rows])
    own = add(stay, send(leave, TO_SIDE))
    mirror = add(kept[:, 0], back_m, near_m)
    away = send(mirror, TO_MIRROR)
    mine = jnp.where(core == side, own, away)
    theirs = jnp.where(core == side, away, own)
    other = send(theirs, TO_CORE)
    left = jnp.where(core == 0, mine, other)
    right = jnp.where(core == 0, other, mine)
    return jnp.concatenate([left, right[:, :, 2 * part - width :]], axis=2).astype(F32)


def rows_out(own, oth):
    width = own.shape[1]
    seen = send(oth, TO_MIRROR)
    both = jnp.concatenate([own.reshape(4, MOST, width), seen.reshape(4, MOST, width)], axis=1)
    here = lax.all_to_all(
        both, "expert", split_axis=0, concat_axis=0, tiled=True, axis_index_groups=Z_GROUPS
    ).reshape(8 * MOST, width)
    return jnp.concatenate([here, send(here, TO_CORE)], axis=0)


def rows_back(partial):
    count, width = partial.shape
    mine, theirs = partial[: count // 2], partial[count // 2 :]
    total = (mine + send(theirs.astype(BF16), TO_CORE).astype(F32)).astype(BF16)
    home = lax.all_to_all(
        total.reshape(4, 2 * MOST, width),
        "expert",
        split_axis=0,
        concat_axis=0,
        tiled=True,
        axis_index_groups=Z_GROUPS,
    )
    own = home[:, :MOST].reshape(4 * MOST, width)
    oth = send(home[:, MOST:].reshape(4 * MOST, width), TO_MIRROR)
    return own, oth


def dot(a, b, over):
    return lax.dot_general(a, b, (over, ((), ())), preferred_element_type=F32)


def on_device(tokens, expert_ids, gate_vals, w_gate, w_up, w_down, cotangent):
    core = lax.axis_index("expert") % 2
    y, x = lax.axis_index("fsdp") // 4, lax.axis_index("fsdp") % 4
    side, low = x // 2, x % 2
    width = w_gate.shape[2]
    place = jnp.stack([y, side]).astype(jnp.int32)
    ids, gates = expert_ids.T, gate_vals.T

    own, oth, gown, goth = dispatch(place, ids, gates, tokens, cotangent)
    gate_up = gather_weights(jnp.concatenate([w_gate, w_up], axis=0), core, side, low)
    down = gather_weights(w_down, core, side, low)[0]
    rows = rows_out(own, oth)
    grads = rows_out(gown, goth)

    gate_pre = dot(rows, gate_up[0], ((1,), (0,)))
    up_pre = dot(rows, gate_up[1], ((1,), (0,)))
    sig = jax.nn.sigmoid(gate_pre)
    hidden = (gate_pre * sig * up_pre).astype(BF16)
    term_down = dot(grads, hidden, ((0,), (0,))).astype(BF16)
    grad_down = scatter_sums(term_down[None], width, core, side, low)
    hidden_grad = dot(grads, down, ((1,), (0,)))
    gate_grad = (hidden_grad * up_pre * sig * (1.0 + gate_pre * (1.0 - sig))).astype(BF16)
    up_grad = (hidden_grad * gate_pre * sig).astype(BF16)
    terms = jnp.stack(
        [
            dot(rows, gate_grad, ((0,), (0,))).astype(BF16),
            dot(rows, up_grad, ((0,), (0,))).astype(BF16),
        ]
    )
    grad_gate_up = scatter_sums(terms, width, core, side, low)
    expert_out = dot(hidden, down, ((1,), (1,)))
    out_own, out_oth = rows_back(expert_out)
    slot_grad = dot(gate_grad, gate_up[0], ((1,), (1,))) + dot(up_grad, gate_up[1], ((1,), (1,)))
    grad_own, grad_oth = rows_back(slot_grad)
    output, grad_tokens, grad_gates = combine(
        place, ids, gates, cotangent, out_own, out_oth, grad_own, grad_oth
    )
    return (output, grad_tokens, grad_gates.T, grad_gate_up[:1], grad_gate_up[1:], grad_down)


def solution(mesh):
    rows, weight = P(AXES, None), P("expert", "fsdp", None)
    return jax.shard_map(
        on_device,
        mesh=mesh,
        in_specs=(rows, rows, rows, weight, weight, weight, rows),
        out_specs=(rows, rows, rows, weight, weight, weight),
        check_vma=False,
    )
```

```python
import functools

import jax
import jax.numpy as jnp
from jax import lax
from jax.experimental import pallas as pl
from jax.experimental.pallas import tpu as pltpu
from jax.sharding import PartitionSpec as P

TOP = 6
MOST = 48
OWNED = 8
LANE = 128
AXES = ("expert", "fsdp")
F32 = jnp.float32
BF16 = jnp.bfloat16


def pairs_of(move):
    pairs = []
    for source in range(128):
        z, core, y, x = source // 32, source // 16 % 2, source // 4 % 4, source % 4
        core, y, x = move(core, y, x)
        pairs.append((source, (z * 2 + core) * 16 + y % 4 * 4 + x))
    return pairs


TO_CORE = pairs_of(lambda core, y, x: (1 - core, y, x))
TO_MIRROR = pairs_of(lambda core, y, x: (core, y, 3 - x))
TO_SIDE = pairs_of(lambda core, y, x: (core, y, x ^ 1))
TO_UP = pairs_of(lambda core, y, x: (core, y + 1, x))
TO_DOWN = pairs_of(lambda core, y, x: (core, y - 1, x))
Z_GROUPS = [[0, 2, 4, 6], [1, 3, 5, 7]]


MOVES = {"core": TO_CORE, "mirror": TO_MIRROR, "side": TO_SIDE, "up": TO_UP, "down": TO_DOWN, "rows": TO_MIRROR}


def after(value, *others):
    return lax.optimization_barrier((value,) + others)[0]


class Rounds:
    def __init__(self):
        self.number, self.held, self.ended, self.ready = 0, [], (), []

    def hold(self, value, rounds=1):
        self.held.append((self.number + rounds, value))
        return value

    def pin(self, value):
        return after(value, *self.ended) if self.ended else value

    def late(self, value):
        return after(value, *self.ready)

    def send(self, link, value, rounds=1):
        value = self.pin(value)
        self.ready.append(value)
        return self.hold(lax.ppermute(value, AXES, MOVES[link]), rounds)

    def exchange(self, value, rounds=1):
        moved = lax.all_to_all(
            value,
            "expert",
            split_axis=0,
            concat_axis=0,
            tiled=True,
            axis_index_groups=Z_GROUPS,
        )
        return self.hold(moved, rounds)

    def next(self):
        self.number += 1
        self.ready = []
        self.ended = tuple(v for due, v in self.held if due == self.number)


def routes(ids, half, own):
    tok_count = ids.shape[1]
    side = half if own else 1 - half
    live = []
    for z in range(4):
        wanted = OWNED * (2 * z + side)
        live.append(jnp.sum(jnp.where(ids == wanted, 1.0, 0.0), axis=0, keepdims=True))
    live = jnp.concatenate(live + [jnp.zeros((4, tok_count), F32)], axis=0)
    before = lax.broadcasted_iota(jnp.int32, (tok_count, tok_count), 0)
    after = lax.broadcasted_iota(jnp.int32, (tok_count, tok_count), 1)
    earlier = jnp.where(before < after, 1.0, 0.0).astype(BF16)
    rank = jnp.dot(live.astype(BF16), earlier, preferred_element_type=F32)
    row = lax.broadcasted_iota(jnp.int32, (MOST, tok_count), 0).astype(F32)
    chosen = []
    for z in range(4):
        here = jnp.where(row == rank[z : z + 1], 1.0, 0.0) * live[z : z + 1]
        chosen.append(here)
    return chosen


def gates_of(ids, gates, half, own):
    side = half if own else 1 - half
    return [
        jnp.sum(jnp.where(ids == OWNED * (2 * z + side), gates, 0.0), axis=0, keepdims=True)
        for z in range(4)
    ]


def dispatch_kernel(place, ids_ref, gates_ref, tok_ref, cot_ref, *outs):
    y, half = place[0], place[1]
    ids = ids_ref[...]
    gates = gates_ref[...].astype(F32)
    width = tok_ref.shape[1] // 8
    for own in (True, False):
        chosen = routes(ids, half, own)
        gate = gates_of(ids, gates, half, own)
        weight = jnp.concatenate(
            [jnp.sum(s * g, axis=1, keepdims=True) for s, g in zip(chosen, gate)], axis=0
        )
        select = jnp.concatenate(chosen, axis=0).astype(BF16)
        side = half if own else 1 - half
        for kind in range(2):
            for step in range(4):
                block = lax.rem(y + step, 4) * 2 + (side if kind == 0 else 1 - side)
                read = pl.ds(pl.multiple_of(block * width, width), width)
                put = slice((kind * 4 + step) * width, (kind * 4 + step + 1) * width)
                rows = jnp.dot(select, tok_ref[:, read], preferred_element_type=F32).astype(BF16)
                cots = jnp.dot(select, cot_ref[:, read], preferred_element_type=F32)
                grads = (weight * cots).astype(BF16)
                if own:
                    for z in range(4):
                        at, part = 2 * z * MOST, slice(z * MOST, (z + 1) * MOST)
                        outs[0][at : at + MOST, put] = rows[part]
                        outs[0][at + MOST : at + 2 * MOST, put] = grads[part]
                else:
                    outs[1][:, put] = rows
                    outs[2][:, put] = grads


def dispatch(place, ids, gates, tokens, cotangent):
    width = tokens.shape[1]
    both = jax.ShapeDtypeStruct((8 * MOST, width), BF16)
    rows = jax.ShapeDtypeStruct((4 * MOST, width), BF16)
    whole = pl.BlockSpec(memory_space=pltpu.VMEM)
    return pl.pallas_call(
        dispatch_kernel,
        out_shape=(both, rows, rows),
        in_specs=[pl.BlockSpec(memory_space=pltpu.SMEM)] + [whole] * 4,
        out_specs=(whole,) * 3,
        compiler_params=pltpu.CompilerParams(vmem_limit_bytes=48 << 20),
        cost_estimate=pl.CostEstimate(
            flops=1_000_000_000, bytes_accessed=6_000_000, transcendentals=0
        ),
        name="dispatch",
    )(place, ids, gates, tokens, cotangent)


TURNED = (((0,), (0,)), ((), ()))


def combine_kernel(
    place, ids_ref, gates_ref, cot_ref, own_ref, oth_ref, gown_ref, goth_ref, out_ref, gtok_ref, gg_ref
):
    y, half = place[0], place[1]
    ids = ids_ref[...]
    gates = gates_ref[...].astype(F32)
    width = cot_ref.shape[1] // 8
    picked, weighted, chosen_of = [], [], []
    for own in (True, False):
        chosen = routes(ids, half, own)
        gate = gates_of(ids, gates, half, own)
        picked.append(jnp.concatenate(chosen, axis=0).astype(BF16))
        weighted.append(
            jnp.concatenate([s * g for s, g in zip(chosen, gate)], axis=0).astype(BF16)
        )
        chosen_of.append(chosen)
    totals = [jnp.zeros((4 * MOST, 1), F32) for _ in range(2)]
    for step in range(4):
        for kind in range(2):
            block = lax.rem(y + step, 4) * 2 + (half if kind == 0 else 1 - half)
            at = pl.ds(pl.multiple_of(block * width, width), width)
            mine = slice((kind * 4 + step) * width, (kind * 4 + step + 1) * width)
            other = slice(((1 - kind) * 4 + step) * width, ((1 - kind) * 4 + step + 1) * width)
            cot = cot_ref[:, at]
            outs = (own_ref[:, mine], oth_ref[:, other])
            grads = (gown_ref[:, mine], goth_ref[:, other])
            out_ref[:, at] = sum(
                lax.dot_general(w, o, TURNED, preferred_element_type=F32)
                for w, o in zip(weighted, outs)
            ).astype(BF16)
            gtok_ref[:, at] = sum(
                lax.dot_general(s, g, TURNED, preferred_element_type=F32)
                for s, g in zip(picked, grads)
            ).astype(BF16)
            for i in range(2):
                cots = jnp.dot(picked[i], cot, preferred_element_type=F32)
                totals[i] += jnp.sum(cots * outs[i].astype(F32), axis=1, keepdims=True)
    result = jnp.zeros(ids.shape, F32)
    for i, own in enumerate((True, False)):
        side = half if own else 1 - half
        for z in range(4):
            per_slot = totals[i][z * MOST : (z + 1) * MOST]
            per_token = jnp.sum(chosen_of[i][z] * per_slot, axis=0, keepdims=True)
            result += jnp.where(ids == OWNED * (2 * z + side), per_token, 0.0)
    gg_ref[...] = result


def combine(place, ids, gates, cotangent, own, oth, gown, goth):
    shape = jax.ShapeDtypeStruct(cotangent.shape, BF16)
    whole = pl.BlockSpec(memory_space=pltpu.VMEM)
    return pl.pallas_call(
        combine_kernel,
        out_shape=(shape, shape, jax.ShapeDtypeStruct(ids.shape, F32)),
        in_specs=[pl.BlockSpec(memory_space=pltpu.SMEM)] + [whole] * 7,
        out_specs=(whole,) * 3,
        compiler_params=pltpu.CompilerParams(vmem_limit_bytes=48 << 20),
        cost_estimate=pl.CostEstimate(
            flops=2_000_000_000, bytes_accessed=8_000_000, transcendentals=0
        ),
        name="combine",
    )(place, ids, gates, cotangent, own, oth, gown, goth)


def half_width(width):
    return -(-width // (2 * LANE)) * LANE


def split_kernel(place, gate_hbm, up_hbm, down_hbm, keep_ref, give_ref, refs, sems):
    hbms = (gate_hbm, up_hbm, down_hbm)
    started = fetch([(hbm.at[0], refs.at[i]) for i, hbm in enumerate(hbms)], sems)
    part = keep_ref.shape[2]
    width = refs.shape[2]
    first = place[3] == 0
    for i, copy in enumerate(started):
        copy.wait()
        left = refs[i, :, :part]
        blank = jnp.zeros((left.shape[0], 2 * part - width), left.dtype)
        right = jnp.concatenate([blank, refs[i, :, part:]], axis=1)
        keep_ref[i] = jnp.where(first, left, right)
        give_ref[i] = jnp.where(first, right, left)


def choose_kernel(place, keep_ref, got_ref, own_gu, own_dn, away_gu, away_dn):
    here = place[3] == place[1]
    for i in range(3):
        own, away, at = (own_gu, away_gu, i) if i < 2 else (own_dn, away_dn, 0)
        own[at] = jnp.where(here, keep_ref[i], got_ref[i])
        away[at] = jnp.where(here, got_ref[i], keep_ref[i])


def in_pair(first, mine, theirs, axis):
    return jnp.where(
        first,
        jnp.concatenate([mine, theirs], axis=axis),
        jnp.concatenate([theirs, mine], axis=axis),
    )


def add(*terms):
    return sum(t.astype(F32) for t in terms).astype(BF16)


def whole_width(mine, other, width, core):
    part = mine.shape[2]
    left = jnp.where(core == 0, mine, other)
    right = jnp.where(core == 0, other, mine)
    return jnp.concatenate([left, right[:, :, 2 * part - width :]], axis=2).astype(F32)


def dot(a, b, over):
    return lax.dot_general(a, b, (over, ((), ())), preferred_element_type=F32)


WIDE = 256


def fetch(copies, sems):
    started = [pltpu.make_async_copy(a, b, sems.at[i]) for i, (a, b) in enumerate(copies)]
    for copy in started:
        copy.start()
    return started


def gate_up_pieces(low, refs, full):
    block0, block1, block2, block3, mir0, mir1, mir3, far, side_a, side_b = refs
    rows = mir0.shape[1]
    copies = [
        (block, full.at[:, pl.ds(2 * rows * i, 2 * rows), :])
        for i, block in enumerate((block0, block1, block2, block3))
    ]
    for i, (mine, theirs) in enumerate(
        (
            (mir0, side_a.at[0:2]),
            (mir1, side_a.at[2:4]),
            (far.at[0:2], side_b.at[2:4]),
            (mir3, side_b.at[0:2]),
        )
    ):
        start = (8 + 2 * i) * rows
        copies.append((mine, full.at[:, pl.ds(start + (1 - low) * rows, rows), :]))
        copies.append((theirs, full.at[:, pl.ds(start + low * rows, rows), :]))
    return copies


def down_pieces(low, refs, full):
    own0, own1, own3, far, side, side_b, block0, block1, block2a, block2b, block3 = refs
    rows = own0.shape[1]
    copies = []
    for i, (mine, theirs) in enumerate(
        (
            (own0.at[0], side.at[0]),
            (own1.at[0], side.at[1]),
            (far.at[2], side_b.at[4]),
            (own3.at[0], side.at[2]),
        )
    ):
        start = 2 * rows * i
        copies.append((mine, full.at[pl.ds(start + low * rows, rows), :]))
        copies.append((theirs, full.at[pl.ds(start + (1 - low) * rows, rows), :]))
    for at, size, block in (
        (8, 2, block0),
        (10, 2, block1),
        (12, 1, block2a),
        (13, 1, block2b),
        (14, 2, block3),
    ):
        copies.append((block.at[0], full.at[pl.ds(at * rows, size * rows), :]))
    return copies


def chunk(i, size=WIDE):
    return pl.ds(pl.multiple_of(i * size, size), size)


def row_pieces(refs, first, full):
    copies = []
    for core, (home, seen) in enumerate((refs[:2], refs[2:])):
        for z in range(4):
            at = (core * 8 + z) * MOST
            copies.append((home.at[z, pl.ds(first, MOST)], full.at[pl.ds(at, MOST)]))
            copies.append((seen.at[z], full.at[pl.ds(at + 4 * MOST, MOST)]))
    return copies


def forward_kernel(place, *refs):
    row_refs, pieces, (hid_ref, fa_ref, fb_ref, rows_ref, full, sems, row_sems) = (
        refs[:4],
        refs[4:14],
        refs[14:],
    )
    started = fetch(row_pieces(row_refs, 0, rows_ref), row_sems)
    started += fetch(gate_up_pieces(place[2], pieces, full), sems)
    for copy in started:
        copy.wait()

    def step(i, unused):
        gate = dot(rows_ref[...], full[0, :, chunk(i)], ((1,), (0,)))
        up = dot(rows_ref[...], full[1, :, chunk(i)], ((1,), (0,)))
        sig = 1.0 / (1.0 + jnp.exp(-gate))
        silu = gate * sig
        hid_ref[:, chunk(i)] = (silu * up).astype(BF16)
        fa_ref[:, chunk(i)] = up * sig * (1.0 + gate * (1.0 - sig))
        fb_ref[:, chunk(i)] = silu
        return unused

    lax.fori_loop(0, hid_ref.shape[1] // WIDE, step, 0)


def term_of(at, rows_ref, right_ref):
    return dot(rows_ref[:, at], right_ref[...], ((0,), (0,))).astype(BF16)


def down_term_kernel(place, hid_ref, *refs):
    row_refs, (keep, give, mir0, mir1, mir2, mir3) = refs[:4], refs[4:10]
    rows_ref, terms, row_sems, sems = refs[10:]
    for copy in fetch(row_pieces(row_refs, MOST, rows_ref), row_sems):
        copy.wait()
    low = place[2]
    rows = keep.shape[1]
    half = terms.shape[0] // 2
    owns, mirs = [], []
    for i in range(4):
        start = 2 * rows * i
        owns.append((terms.at[pl.ds(start + low * rows, rows), :], keep.at[i]))
        owns.append((terms.at[pl.ds(start + (1 - low) * rows, rows), :], give.at[i]))
    for i, mir in enumerate((mir0, mir1, mir2, mir3)):
        mirs.append((terms.at[pl.ds(half + 2 * i * rows, 2 * rows), :], mir.at[0]))
    terms[:half, :] = term_of(slice(0, half), rows_ref, hid_ref)
    started = fetch(owns, sems)
    terms[half:, :] = term_of(slice(half, 2 * half), rows_ref, hid_ref)
    started += fetch(mirs, row_sems)
    for copy in started:
        copy.wait()


def gradient_kernel(place, fa_ref, fb_ref, *refs):
    grad_refs, tok_refs, pieces, refs = refs[:4], refs[4:8], refs[8:19], refs[19:]
    both_ref, blk0, blk1, blk2, blk3, keep, give_a, give_b = refs[:8]
    g_rows, x_rows, full, terms, in_sems, out_sems, g_sems, x_sems = refs[8:]
    low = place[2]
    rows = give_b.shape[2]
    started = fetch(row_pieces(grad_refs, MOST, g_rows), g_sems)
    started += fetch(down_pieces(low, pieces, full), in_sems)
    later = fetch(row_pieces(tok_refs, 0, x_rows), x_sems)
    for copy in started:
        copy.wait()

    def step(i, unused):
        hidden_grad = dot(g_rows[...], full[:, chunk(i)], ((1,), (0,)))
        both_ref[0, :, chunk(i)] = (hidden_grad * fa_ref[:, chunk(i)]).astype(BF16)
        both_ref[1, :, chunk(i)] = (hidden_grad * fb_ref[:, chunk(i)]).astype(BF16)
        return unused

    lax.fori_loop(0, both_ref.shape[2] // WIDE, step, 0)
    for copy in later:
        copy.wait()

    half = terms.shape[1] // 2
    blocks, mirs = [], []
    for i, blk in enumerate((blk0, blk1, blk2, blk3)):
        blocks.append((terms.at[:, pl.ds(2 * rows * i, 2 * rows), :], blk))
    for i, give in enumerate((give_b.at[0], give_a.at[1], give_a.at[0], give_b.at[1])):
        start = (8 + 2 * i) * rows
        mirs.append((terms.at[:, pl.ds(start + (1 - low) * rows, rows), :], keep.at[i]))
        mirs.append((terms.at[:, pl.ds(start + low * rows, rows), :], give))
    started = []
    for copies, first, sems in ((blocks, 0, in_sems), (mirs, half, out_sems)):
        at = slice(first, first + half)

        def put(i, unused, at=at):
            terms[i, at, :] = dot(x_rows[:, at], both_ref[i], ((0,), (0,))).astype(BF16)
            return unused

        lax.fori_loop(0, 2, put, 0)
        started += fetch(copies, sems)
    for copy in started:
        copy.wait()


def output_kernel(place, hid_ref, both_ref, *refs):
    up_pieces, dn_pieces, refs = refs[:10], refs[10:21], refs[21:]
    out_mine, grad_mine, theirs, full, down, sems, down_sems = refs
    low = place[2]
    first = fetch(down_pieces(low, dn_pieces, down), down_sems)
    second = fetch(gate_up_pieces(low, up_pieces, full), sems)
    count = out_mine.shape[0]
    for copy in first:
        copy.wait()

    half = down.shape[0] // 2

    def out_step(i, unused):
        at = chunk(i, half)
        out_mine[:, at] = dot(hid_ref[:count, :], down[at, :], ((1,), (1,)))
        theirs[:count, at] = dot(hid_ref[count:, :], down[at, :], ((1,), (1,))).astype(BF16)
        return unused

    lax.fori_loop(0, 2, out_step, 0)
    for copy in second:
        copy.wait()

    def grad_step(i, unused):
        at = chunk(i, half)
        gate, up = full[0, at, :], full[1, at, :]
        for mine, to in ((slice(0, count), grad_mine), (slice(count, 2 * count), theirs)):
            total = dot(both_ref[0, mine, :], gate, ((1,), (1,))) + dot(
                both_ref[1, mine, :], up, ((1,), (1,))
            )
            to[mine if to is theirs else slice(None), at] = total.astype(to.dtype)
        return unused

    lax.fori_loop(0, 2, grad_step, 0)


def run(kernel, name, place, local, remote, outs, far_outs, scratch, flops):
    vmem, anywhere = pl.BlockSpec(memory_space=pltpu.VMEM), pl.BlockSpec(memory_space=pl.ANY)
    shapes = [jax.ShapeDtypeStruct(*o) for o in tuple(outs) + tuple(far_outs)]
    size = sum(a.size * a.dtype.itemsize for a in (*local, *remote))
    size += sum(a.size * a.dtype.itemsize for a in shapes)
    return pl.pallas_call(
        kernel,
        out_shape=shapes,
        in_specs=[pl.BlockSpec(memory_space=pltpu.SMEM)]
        + [vmem] * len(local)
        + [anywhere] * len(remote),
        out_specs=[vmem] * len(outs) + [anywhere] * len(far_outs),
        scratch_shapes=scratch,
        compiler_params=pltpu.CompilerParams(vmem_limit_bytes=44 << 20),
        cost_estimate=pl.CostEstimate(
            flops=flops, bytes_accessed=size, transcendentals=0
        ),
        name=name,
    )(place, *local, *remote)


def on_device(tokens, expert_ids, gate_vals, w_gate, w_up, w_down, cotangent):
    core = lax.axis_index("expert") % 2
    y, x = lax.axis_index("fsdp") // 4, lax.axis_index("fsdp") % 4
    side, low = x // 2, x % 2
    rows, width = w_gate.shape[1:]
    depth = tokens.shape[1]
    part = half_width(width)
    quarter = 4 * MOST
    count = 4 * quarter
    work = count * depth * part * 2
    dma, row_dma = pltpu.SemaphoreType.DMA((13,)), pltpu.SemaphoreType.DMA((16,))
    row_scratch = pltpu.VMEM((count, depth), BF16)
    place = jnp.stack([y, side, low, core]).astype(jnp.int32)
    ids, gates = expert_ids.T, gate_vals.T
    r = Rounds()
    send = r.send

    def join(*arrays):
        return jnp.concatenate(arrays, axis=0)

    slices = ((3, rows, part), BF16)
    keep, give = run(
        split_kernel,
        "split",
        place,
        (),
        (w_gate, w_up, w_down),
        [slices] * 2,
        [],
        [pltpu.VMEM((3, rows, width), BF16), pltpu.SemaphoreType.DMA((3,))],
        1,
    )
    got = send("core", give)
    own_gu, own_dn, away_gu, away_dn = run(
        choose_kernel,
        "choose",
        place,
        (keep, got),
        (),
        [((2, rows, part), BF16), ((1, rows, part), BF16)] * 2,
        [],
        [],
        1,
    )
    r.next()
    side_gu = send("side", own_gu)
    mir0 = send("mirror", away_gu)
    own3 = send("up", own_dn)
    own1 = send("down", own_dn)
    r.next()
    block0 = in_pair(low == 0, own_gu, side_gu, 1)
    mir3 = send("up", mir0)
    mir1 = send("down", mir0)
    dn_mir = send("mirror", away_dn)
    both, oth, goth = dispatch(r.late(place), ids, gates, tokens, cotangent)
    home = r.exchange(r.late(both).reshape(4, 2 * MOST, depth), 2)
    r.next()
    block3 = send("up", block0)
    far = send("down", join(mir1, own1))
    side_a = send("side", join(mir0, mir1, dn_mir))
    tok_mir = send("mirror", oth)
    r.next()
    block_dn = in_pair(low == 1, dn_mir, side_a[4:], 1)
    block2 = send("up", block3)
    block1 = send("down", block0)
    side_b = send("side", join(mir3, far))
    grad_mir = send("mirror", goth)
    home_got = r.hold(lax.ppermute(r.late(home), AXES, TO_CORE))
    seen_tok = r.exchange(tok_mir.reshape(4, MOST, depth), 2)
    r.next()
    dn3 = send("up", block_dn)
    dn1 = send("down", block_dn)
    own_side = send("side", join(own_dn, own1, own3))
    tok_got = r.hold(lax.ppermute(after(seen_tok, side_b), AXES, TO_CORE))
    token_rows = (home, seen_tok, home_got, tok_got)
    gu_pieces = (block0, block1, block2, block3, mir0, mir1, mir3, far, side_a, side_b)
    hidden, fa, fb = run(
        forward_kernel,
        "forward",
        r.late(place),
        (),
        token_rows + gu_pieces,
        [((count, part), BF16), ((count, part), F32), ((count, part), F32)],
        [],
        [row_scratch, pltpu.VMEM((2, depth, part), BF16), dma, row_dma],
        2 * work,
    )
    r.hold(hidden)
    seen_grad = r.exchange(r.late(grad_mir).reshape(4, MOST, depth))
    r.next()
    dn2a = send("up", r.pin(dn3)[:, :rows])
    dn2b = send("down", r.pin(dn1)[:, rows:])
    grad_got = r.hold(lax.ppermute(r.pin(seen_grad), AXES, TO_CORE))
    grad_rows = (home, seen_grad, home_got, grad_got)
    own_keep, own_give, mir_t0, mir_t1, mir_t2, mir_t3 = run(
        down_term_kernel,
        "down_term",
        place,
        (r.pin(hidden),),
        grad_rows,
        [],
        [((4, rows, part), BF16)] * 2 + [((1, 2 * rows, part), BF16)] * 4,
        [row_scratch, pltpu.VMEM((depth, part), BF16), row_dma, dma],
        work,
    )
    r.hold(own_give)
    r.next()
    dn_pieces = (own_dn, own1, own3, far, own_side, side_b, block_dn, dn1, dn2a, dn2b, dn3)
    dn_far = send("down", mir_t2)
    dn_back = send("up", mir_t1)
    own_got = send("side", own_give)
    hidden_grads, blk_t0, blk_t1, blk_t2, blk_t3, mir_keep, give_a, give_b = run(
        gradient_kernel,
        "gradient",
        place,
        (r.pin(fa), fb),
        grad_rows + token_rows + dn_pieces,
        [((2, count, part), BF16)],
        [((2, 2 * rows, part), BF16)] * 4
        + [((4, 2, rows, part), BF16)]
        + [((2, 2, rows, part), BF16)] * 2,
        [row_scratch, row_scratch]
        + [pltpu.VMEM((depth, part), BF16), pltpu.VMEM((2, depth, part), BF16)]
        + [dma, dma, row_dma, row_dma],
        3 * work,
    )
    r.hold(give_a)

    r.next()
    own_sum = add(own_keep, own_got)
    blk_far = send("up", blk_t2)
    blk_back = send("down", blk_t3)
    got_a = send("side", give_a)
    own_far = send("down", own_sum[2:3])
    out_mine, grad_mine, theirs = run(
        output_kernel,
        "outputs",
        place,
        (r.pin(hidden), hidden_grads),
        gu_pieces + dn_pieces,
        [((count // 2, depth), F32)] * 2 + [((count, depth), BF16)],
        [],
        [pltpu.VMEM((2, depth, part), BF16), pltpu.VMEM((depth, part), BF16), dma, dma],
        3 * work,
    )
    r.hold(theirs)
    r.next()
    blk_near = send("up", add(blk_far, blk_t1))
    mir_far = send("down", add(mir_keep[2], got_a[0]))
    got_b = send("side", give_b)
    dn_down = send(
        "down", jnp.concatenate([add(dn_far, mir_t3), add(own_far, own_sum[3:])], axis=1)
    )
    got = send("core", theirs)
    out = r.hold(add(r.late(out_mine), got[: 2 * quarter]))
    out_home = r.exchange(out[quarter:].reshape(4, MOST, depth))
    grd = r.hold(add(r.late(grad_mine), got[2 * quarter :]))
    grad_home = r.exchange(grd[quarter:].reshape(4, MOST, depth), 2)
    r.next()
    dn_down, blk_near, blk_back = r.pin(dn_down), r.pin(blk_near), r.pin(blk_back)
    dn_near, own_near = dn_down[:, : 2 * rows], dn_down[:, 2 * rows :]
    mir_back = send("up", jnp.concatenate([add(mir_keep[1], got_a[1]), own_sum[1:2]], axis=0))
    mir_near = send("down", add(r.pin(mir_far), mir_keep[3], r.pin(got_b)[1]))
    blk = add(blk_t0, blk_back, blk_near)
    mir_dn = add(mir_t0, dn_back, dn_near)
    low_half, high_half = join(blk[:, :rows], mir_dn[:, rows:]), join(blk[:, rows:], mir_dn[:, :rows])
    stay = jnp.where(low == 0, low_half, high_half)
    leave_got = send("side", jnp.where(low == 0, high_half, low_half))
    out_oth = send("mirror", out_home.reshape(quarter, depth))
    out_own = r.exchange(r.late(out[:quarter]).reshape(4, MOST, depth), 2)
    r.next()
    here = core == side
    mir_back = r.pin(mir_back)
    mine = add(stay, r.pin(leave_got))
    gu_mir = add(mir_keep[0], got_b[0], mir_back[:2], r.pin(mir_near))
    away = send("mirror", join(gu_mir, mine[2:]))
    grad_oth = send("mirror", grad_home.reshape(quarter, depth))
    grad_own = r.exchange(r.late(grd[:quarter]).reshape(4, MOST, depth))
    out_own, grad_own = out_own.reshape(quarter, depth), grad_own.reshape(quarter, depth)
    own = join(mine[:2], add(own_sum[:1], mir_back[2:], own_near))
    other = lax.ppermute(jnp.where(here, away, own), AXES, TO_CORE)
    kept = jnp.where(here, own, away)
    grad_gate, grad_up, grad_down = (
        whole_width(kept[i : i + 1], other[i : i + 1], width, core) for i in range(3)
    )

    output, grad_tokens, grad_gates = combine(
        place, ids, gates, cotangent, out_own, out_oth, grad_own, grad_oth
    )
    return (output, grad_tokens, grad_gates.T, grad_gate, grad_up, grad_down)


def solution(mesh):
    rows, weight = P(AXES, None), P("expert", "fsdp", None)
    return jax.shard_map(
        on_device,
        mesh=mesh,
        in_specs=(rows, rows, rows, weight, weight, weight, rows),
        out_specs=(rows, rows, rows, weight, weight, weight),
        check_vma=False,
    )
```

```python
import functools

import jax
import jax.numpy as jnp
from jax import lax
from jax.experimental import pallas as pl
from jax.experimental.pallas import tpu as pltpu
from jax.sharding import PartitionSpec as P

TOP = 6
MOST = 48
OWNED = 8
LANE = 128
AXES = ("expert", "fsdp")
F32 = jnp.float32
BF16 = jnp.bfloat16


def pairs_of(move):
    pairs = []
    for source in range(128):
        z, core, y, x = source // 32, source // 16 % 2, source // 4 % 4, source % 4
        core, y, x = move(core, y, x)
        pairs.append((source, (z * 2 + core) * 16 + y % 4 * 4 + x))
    return pairs


TO_CORE = pairs_of(lambda core, y, x: (1 - core, y, x))
TO_MIRROR = pairs_of(lambda core, y, x: (core, y, 3 - x))
TO_SIDE = pairs_of(lambda core, y, x: (core, y, x ^ 1))
TO_UP = pairs_of(lambda core, y, x: (core, y + 1, x))
TO_DOWN = pairs_of(lambda core, y, x: (core, y - 1, x))
Z_GROUPS = [[0, 2, 4, 6], [1, 3, 5, 7]]


MOVES = {"core": TO_CORE, "mirror": TO_MIRROR, "side": TO_SIDE, "up": TO_UP, "down": TO_DOWN, "rows": TO_MIRROR}


def after(value, *others):
    return lax.optimization_barrier((value,) + others)[0]


class Rounds:
    def __init__(self):
        self.number, self.held, self.ended, self.ready = 0, [], (), []

    def hold(self, value, rounds=1):
        self.held.append((self.number + rounds, value))
        return value

    def pin(self, value):
        return after(value, *self.ended) if self.ended else value

    def late(self, value):
        return after(value, *self.ready)

    def send(self, link, value, rounds=1):
        value = self.pin(value)
        self.ready.append(value)
        return self.hold(lax.ppermute(value, AXES, MOVES[link]), rounds)

    def exchange(self, value, rounds=1):
        moved = lax.all_to_all(
            value,
            "expert",
            split_axis=0,
            concat_axis=0,
            tiled=True,
            axis_index_groups=Z_GROUPS,
        )
        return self.hold(moved, rounds)

    def next(self):
        self.number += 1
        self.ready = []
        self.ended = tuple(v for due, v in self.held if due == self.number)


def routes(ids, half, own):
    tok_count = ids.shape[1]
    side = half if own else 1 - half
    live = []
    for z in range(4):
        wanted = OWNED * (2 * z + side)
        live.append(jnp.sum(jnp.where(ids == wanted, 1.0, 0.0), axis=0, keepdims=True))
    live = jnp.concatenate(live + [jnp.zeros((4, tok_count), F32)], axis=0)
    before = lax.broadcasted_iota(jnp.int32, (tok_count, tok_count), 0)
    after = lax.broadcasted_iota(jnp.int32, (tok_count, tok_count), 1)
    earlier = jnp.where(before < after, 1.0, 0.0).astype(BF16)
    rank = jnp.dot(live.astype(BF16), earlier, preferred_element_type=F32)
    row = lax.broadcasted_iota(jnp.int32, (MOST, tok_count), 0).astype(F32)
    chosen = []
    for z in range(4):
        here = jnp.where(row == rank[z : z + 1], 1.0, 0.0) * live[z : z + 1]
        chosen.append(here)
    return chosen


def gates_of(ids, gates, half, own):
    side = half if own else 1 - half
    return [
        jnp.sum(jnp.where(ids == OWNED * (2 * z + side), gates, 0.0), axis=0, keepdims=True)
        for z in range(4)
    ]


def dispatch_kernel(place, ids_ref, gates_ref, tok_ref, cot_ref, *outs):
    y, half = place[0], place[1]
    ids = ids_ref[...]
    gates = gates_ref[...].astype(F32)
    width = tok_ref.shape[1] // 8
    for own in (True, False):
        chosen = routes(ids, half, own)
        gate = gates_of(ids, gates, half, own)
        weight = jnp.concatenate(
            [jnp.sum(s * g, axis=1, keepdims=True) for s, g in zip(chosen, gate)], axis=0
        )
        select = jnp.concatenate(chosen, axis=0).astype(BF16)
        side = half if own else 1 - half
        for kind in range(2):

            def fill(step, unused, own=own, kind=kind, side=side, select=select, weight=weight):
                block = lax.rem(y + step, 4) * 2 + (side if kind == 0 else 1 - side)
                read = pl.ds(pl.multiple_of(block * width, width), width)
                put = pl.ds(pl.multiple_of((kind * 4 + step) * width, width), width)
                rows = jnp.dot(select, tok_ref[:, read], preferred_element_type=F32).astype(BF16)
                cots = jnp.dot(select, cot_ref[:, read], preferred_element_type=F32)
                grads = (weight * cots).astype(BF16)
                if own:
                    for z in range(4):
                        at, part = 2 * z * MOST, slice(z * MOST, (z + 1) * MOST)
                        outs[0][at : at + MOST, put] = rows[part]
                        outs[0][at + MOST : at + 2 * MOST, put] = grads[part]
                else:
                    outs[1][:, put] = rows
                    outs[2][:, put] = grads
                return unused

            lax.fori_loop(0, 4, fill, 0)


def dispatch(place, ids, gates, tokens, cotangent):
    width = tokens.shape[1]
    both = jax.ShapeDtypeStruct((8 * MOST, width), BF16)
    rows = jax.ShapeDtypeStruct((4 * MOST, width), BF16)
    whole = pl.BlockSpec(memory_space=pltpu.VMEM)
    return pl.pallas_call(
        dispatch_kernel,
        out_shape=(both, rows, rows),
        in_specs=[pl.BlockSpec(memory_space=pltpu.SMEM)] + [whole] * 4,
        out_specs=(whole,) * 3,
        compiler_params=pltpu.CompilerParams(vmem_limit_bytes=48 << 20),
        cost_estimate=pl.CostEstimate(
            flops=1_000_000_000, bytes_accessed=6_000_000, transcendentals=0
        ),
        name="dispatch",
    )(place, ids, gates, tokens, cotangent)


TURNED = (((0,), (0,)), ((), ()))


def combine_kernel(
    place, ids_ref, gates_ref, cot_ref, own_ref, oth_ref, gown_ref, goth_ref, out_ref, gtok_ref, gg_ref
):
    y, half = place[0], place[1]
    ids = ids_ref[...]
    gates = gates_ref[...].astype(F32)
    width = cot_ref.shape[1] // 8
    picked, weighted, chosen_of = [], [], []
    for own in (True, False):
        chosen = routes(ids, half, own)
        gate = gates_of(ids, gates, half, own)
        picked.append(jnp.concatenate(chosen, axis=0).astype(BF16))
        weighted.append(
            jnp.concatenate([s * g for s, g in zip(chosen, gate)], axis=0).astype(BF16)
        )
        chosen_of.append(chosen)
    def step_of(step, totals):
        totals = list(totals)
        for kind in range(2):
            block = lax.rem(y + step, 4) * 2 + (half if kind == 0 else 1 - half)
            at = pl.ds(pl.multiple_of(block * width, width), width)
            mine = pl.ds(pl.multiple_of((kind * 4 + step) * width, width), width)
            other = pl.ds(pl.multiple_of(((1 - kind) * 4 + step) * width, width), width)
            cot = cot_ref[:, at]
            outs = (own_ref[:, mine], oth_ref[:, other])
            grads = (gown_ref[:, mine], goth_ref[:, other])
            out_ref[:, at] = sum(
                lax.dot_general(w, o, TURNED, preferred_element_type=F32)
                for w, o in zip(weighted, outs)
            ).astype(BF16)
            gtok_ref[:, at] = sum(
                lax.dot_general(s, g, TURNED, preferred_element_type=F32)
                for s, g in zip(picked, grads)
            ).astype(BF16)
            for i in range(2):
                cots = jnp.dot(picked[i], cot, preferred_element_type=F32)
                totals[i] += jnp.sum(cots * outs[i].astype(F32), axis=1, keepdims=True)
        return tuple(totals)

    zero = jnp.zeros((4 * MOST, 1), F32)
    totals = lax.fori_loop(0, 4, step_of, (zero, zero))
    result = jnp.zeros(ids.shape, F32)
    for i, own in enumerate((True, False)):
        side = half if own else 1 - half
        for z in range(4):
            per_slot = totals[i][z * MOST : (z + 1) * MOST]
            per_token = jnp.sum(chosen_of[i][z] * per_slot, axis=0, keepdims=True)
            result += jnp.where(ids == OWNED * (2 * z + side), per_token, 0.0)
    gg_ref[...] = result


def combine(place, ids, gates, cotangent, own, oth, gown, goth):
    shape = jax.ShapeDtypeStruct(cotangent.shape, BF16)
    whole = pl.BlockSpec(memory_space=pltpu.VMEM)
    return pl.pallas_call(
        combine_kernel,
        out_shape=(shape, shape, jax.ShapeDtypeStruct(ids.shape, F32)),
        in_specs=[pl.BlockSpec(memory_space=pltpu.SMEM)] + [whole] * 7,
        out_specs=(whole,) * 3,
        compiler_params=pltpu.CompilerParams(vmem_limit_bytes=48 << 20),
        cost_estimate=pl.CostEstimate(
            flops=2_000_000_000, bytes_accessed=8_000_000, transcendentals=0
        ),
        name="combine",
    )(place, ids, gates, cotangent, own, oth, gown, goth)


def half_width(width):
    return -(-width // (2 * LANE)) * LANE


def split_kernel(place, gate_hbm, up_hbm, down_hbm, keep_ref, give_ref, refs, sems):
    hbms = (gate_hbm, up_hbm, down_hbm)
    started = fetch([(hbm.at[0], refs.at[i]) for i, hbm in enumerate(hbms)], sems)
    part = keep_ref.shape[2]
    width = refs.shape[2]
    first = place[3] == 0
    for i, copy in enumerate(started):
        copy.wait()
        left = refs[i, :, :part]
        blank = jnp.zeros((left.shape[0], 2 * part - width), left.dtype)
        right = jnp.concatenate([blank, refs[i, :, part:]], axis=1)
        keep_ref[i] = jnp.where(first, left, right)
        give_ref[i] = jnp.where(first, right, left)


def choose_kernel(place, keep_ref, got_ref, own_gu, own_dn, away_gu, away_dn):
    here = place[3] == place[1]
    for i in range(3):
        own, away, at = (own_gu, away_gu, i) if i < 2 else (own_dn, away_dn, 0)
        own[at] = jnp.where(here, keep_ref[i], got_ref[i])
        away[at] = jnp.where(here, got_ref[i], keep_ref[i])


def in_pair(first, mine, theirs, axis):
    return jnp.where(
        first,
        jnp.concatenate([mine, theirs], axis=axis),
        jnp.concatenate([theirs, mine], axis=axis),
    )


def add(*terms):
    return sum(t.astype(F32) for t in terms).astype(BF16)


def dot(a, b, over):
    return lax.dot_general(a, b, (over, ((), ())), preferred_element_type=F32)


WIDE = 256


def fetch(copies, sems):
    started = [pltpu.make_async_copy(a, b, sems.at[i]) for i, (a, b) in enumerate(copies)]
    for copy in started:
        copy.start()
    return started


def gate_up_pieces(low, refs, full):
    block0, block1, block2, block3, mir0, mir1, mir3, far, side_a, side_b = refs
    rows = mir0.shape[1]
    copies = [
        (block, full.at[:, pl.ds(2 * rows * i, 2 * rows), :])
        for i, block in enumerate((block0, block1, block2, block3))
    ]
    for i, (mine, theirs) in enumerate(
        (
            (mir0, side_a.at[0:2]),
            (mir1, side_a.at[2:4]),
            (far.at[0:2], side_b.at[2:4]),
            (mir3, side_b.at[0:2]),
        )
    ):
        start = (8 + 2 * i) * rows
        copies.append((mine, full.at[:, pl.ds(start + (1 - low) * rows, rows), :]))
        copies.append((theirs, full.at[:, pl.ds(start + low * rows, rows), :]))
    return copies


def down_pieces(low, refs, full):
    own0, own1, own3, far, side, side_b, block0, block1, block2a, block2b, block3 = refs
    rows = own0.shape[1]
    copies = []
    for i, (mine, theirs) in enumerate(
        (
            (own0.at[0], side.at[0]),
            (own1.at[0], side.at[1]),
            (far.at[2], side_b.at[4]),
            (own3.at[0], side.at[2]),
        )
    ):
        start = 2 * rows * i
        copies.append((mine, full.at[pl.ds(start + low * rows, rows), :]))
        copies.append((theirs, full.at[pl.ds(start + (1 - low) * rows, rows), :]))
    for at, size, block in (
        (8, 2, block0),
        (10, 2, block1),
        (12, 1, block2a),
        (13, 1, block2b),
        (14, 2, block3),
    ):
        copies.append((block.at[0], full.at[pl.ds(at * rows, size * rows), :]))
    return copies


def chunk(i, size=WIDE):
    return pl.ds(pl.multiple_of(i * size, size), size)


def row_pieces(refs, first, full):
    copies = []
    for core, (home, seen) in enumerate((refs[:2], refs[2:])):
        for z in range(4):
            at = (core * 8 + z) * MOST
            copies.append((home.at[z, pl.ds(first, MOST)], full.at[pl.ds(at, MOST)]))
            copies.append((seen.at[z], full.at[pl.ds(at + 4 * MOST, MOST)]))
    return copies


def forward_kernel(place, *refs):
    row_refs, pieces, (hid_ref, fa_ref, fb_ref, rows_ref, full, sems, row_sems) = (
        refs[:4],
        refs[4:14],
        refs[14:],
    )
    started = fetch(row_pieces(row_refs, 0, rows_ref), row_sems)
    started += fetch(gate_up_pieces(place[2], pieces, full), sems)
    for copy in started:
        copy.wait()

    def step(i, unused):
        gate = dot(rows_ref[...], full[0, :, chunk(i)], ((1,), (0,)))
        up = dot(rows_ref[...], full[1, :, chunk(i)], ((1,), (0,)))
        sig = 1.0 / (1.0 + jnp.exp(-gate))
        silu = gate * sig
        hid_ref[:, chunk(i)] = (silu * up).astype(BF16)
        fa_ref[:, chunk(i)] = up * sig * (1.0 + gate * (1.0 - sig))
        fb_ref[:, chunk(i)] = silu
        return unused

    lax.fori_loop(0, hid_ref.shape[1] // WIDE, step, 0)


def term_of(at, rows_ref, right_ref):
    return dot(rows_ref[:, at], right_ref[...], ((0,), (0,))).astype(BF16)


def down_term_kernel(place, hid_ref, *refs):
    row_refs, (keep, give, mir0, mir1, mir2, mir3) = refs[:4], refs[4:10]
    rows_ref, terms, row_sems, sems = refs[10:]
    for copy in fetch(row_pieces(row_refs, MOST, rows_ref), row_sems):
        copy.wait()
    low = place[2]
    rows = keep.shape[1]
    half = terms.shape[0] // 2
    owns, mirs = [], []
    for i in range(4):
        start = 2 * rows * i
        owns.append((terms.at[pl.ds(start + low * rows, rows), :], keep.at[i]))
        owns.append((terms.at[pl.ds(start + (1 - low) * rows, rows), :], give.at[i]))
    for i, mir in enumerate((mir0, mir1, mir2, mir3)):
        mirs.append((terms.at[pl.ds(half + 2 * i * rows, 2 * rows), :], mir.at[0]))
    terms[:half, :] = term_of(slice(0, half), rows_ref, hid_ref)
    started = fetch(owns, sems)
    terms[half:, :] = term_of(slice(half, 2 * half), rows_ref, hid_ref)
    started += fetch(mirs, row_sems)
    for copy in started:
        copy.wait()


def gradient_kernel(place, fa_ref, fb_ref, *refs):
    grad_refs, tok_refs, pieces, refs = refs[:4], refs[4:8], refs[8:19], refs[19:]
    both_ref, blk0, blk1, blk2, blk3, keep, give_a, give_b = refs[:8]
    g_rows, x_rows, full, terms, in_sems, out_sems, g_sems, x_sems = refs[8:]
    low = place[2]
    rows = give_b.shape[2]
    started = fetch(row_pieces(grad_refs, MOST, g_rows), g_sems)
    started += fetch(down_pieces(low, pieces, full), in_sems)
    later = fetch(row_pieces(tok_refs, 0, x_rows), x_sems)
    for copy in started:
        copy.wait()

    def step(i, unused):
        hidden_grad = dot(g_rows[...], full[:, chunk(i)], ((1,), (0,)))
        both_ref[0, :, chunk(i)] = (hidden_grad * fa_ref[:, chunk(i)]).astype(BF16)
        both_ref[1, :, chunk(i)] = (hidden_grad * fb_ref[:, chunk(i)]).astype(BF16)
        return unused

    lax.fori_loop(0, both_ref.shape[2] // WIDE, step, 0)
    for copy in later:
        copy.wait()

    half = terms.shape[1] // 2
    blocks, mirs = [], []
    for i, blk in enumerate((blk0, blk1, blk2, blk3)):
        blocks.append((terms.at[:, pl.ds(2 * rows * i, 2 * rows), :], blk))
    for i, give in enumerate((give_b.at[0], give_a.at[1], give_a.at[0], give_b.at[1])):
        start = (8 + 2 * i) * rows
        mirs.append((terms.at[:, pl.ds(start + (1 - low) * rows, rows), :], keep.at[i]))
        mirs.append((terms.at[:, pl.ds(start + low * rows, rows), :], give))
    started = []
    for copies, first, sems in ((blocks, 0, in_sems), (mirs, half, out_sems)):
        at = slice(first, first + half)

        def put(i, unused, at=at):
            terms[i, at, :] = dot(x_rows[:, at], both_ref[i], ((0,), (0,))).astype(BF16)
            return unused

        lax.fori_loop(0, 2, put, 0)
        started += fetch(copies, sems)
    for copy in started:
        copy.wait()


def output_kernel(place, hid_ref, both_ref, *refs):
    up_pieces, dn_pieces, refs = refs[:10], refs[10:21], refs[21:]
    out_mine, grad_mine, theirs, full, down, sems, down_sems = refs
    low = place[2]
    first = fetch(down_pieces(low, dn_pieces, down), down_sems)
    second = fetch(gate_up_pieces(low, up_pieces, full), sems)
    count = out_mine.shape[0]
    for copy in first:
        copy.wait()

    half = down.shape[0] // 2

    def out_step(i, unused):
        at = chunk(i, half)
        out_mine[:, at] = dot(hid_ref[:count, :], down[at, :], ((1,), (1,)))
        theirs[:count, at] = dot(hid_ref[count:, :], down[at, :], ((1,), (1,))).astype(BF16)
        return unused

    lax.fori_loop(0, 2, out_step, 0)
    for copy in second:
        copy.wait()

    def grad_step(i, unused):
        at = chunk(i, half)
        gate, up = full[0, at, :], full[1, at, :]
        for mine, to in ((slice(0, count), grad_mine), (slice(count, 2 * count), theirs)):
            total = dot(both_ref[0, mine, :], gate, ((1,), (1,))) + dot(
                both_ref[1, mine, :], up, ((1,), (1,))
            )
            to[mine if to is theirs else slice(None), at] = total.astype(to.dtype)
        return unused

    lax.fori_loop(0, 2, grad_step, 0)


STEP = 64


def sum_rows(to, *terms):
    def step(i, unused):
        at = chunk(i, STEP)
        to[at, :] = sum(t[at, :].astype(F32) for t in terms).astype(to.dtype)
        return unused

    lax.fori_loop(0, to.shape[0] // STEP, step, 0)


def near_kernel(place, blk_far, blk1, keep, got_a, dn_far, mir3, own_far, own_sum, blk, mir, dn):
    size = mir3.shape[1]
    for g in range(2):
        sum_rows(blk.at[g], blk_far.at[g], blk1.at[g])
        sum_rows(mir.at[g], keep.at[2, g], got_a.at[0, g])
    sum_rows(dn.at[0, 0:size], dn_far.at[0], mir3.at[0])
    sum_rows(dn.at[0, size:], own_far.at[0], own_sum.at[3])


def cross_kernel(place, blk0, blk_back, blk_near, mir0, dn_back, dn_down, *refs):
    keep, got_a, got_b, mir_far, own_sum, stay, leave, up, down = refs
    low = place[2]
    rows = stay.shape[1]
    first, second = pl.ds(low * rows, rows), pl.ds((1 - low) * rows, rows)
    for g in range(2):
        for to, at in ((stay, first), (leave, second)):
            sum_rows(to.at[g], blk0.at[g, at], blk_back.at[g, at], blk_near.at[g, at])
        sum_rows(up.at[g], keep.at[1, g], got_a.at[1, g])
        sum_rows(down.at[g], mir_far.at[g], keep.at[3, g], got_b.at[1, g])
    for to, at in ((stay, second), (leave, first)):
        sum_rows(to.at[2], mir0.at[0, at], dn_back.at[0, at], dn_down.at[0, at])
    sum_rows(up.at[2], own_sum.at[1])


def last_kernel(place, stay, leave_got, keep, got_b, up, mir_near, own_sum, dn_down, mir, own):
    rows = stay.shape[1]
    for g in range(2):
        sum_rows(mir.at[g], keep.at[0, g], got_b.at[0, g], up.at[g], mir_near.at[g])
        sum_rows(own.at[g], stay.at[g], leave_got.at[g])
    sum_rows(mir.at[2], stay.at[2], leave_got.at[2])
    sum_rows(own.at[2], own_sum.at[0], up.at[2], dn_down.at[0, 2 * rows :])


def pick_kernel(place, own, away, keep_ref, give_ref):
    here = place[3] == place[1]
    for i in range(3):
        keep_ref[i] = jnp.where(here, own[i], away[i])
        give_ref[i] = jnp.where(here, away[i], own[i])


def widen_kernel(place, keep, got, *outs):
    first = place[3] == 0
    part = keep.shape[2]
    for i, out in enumerate(outs):
        extra = 2 * part - out.shape[2]
        out[0, :, :part] = jnp.where(first, keep[i], got[i]).astype(F32)
        out[0, :, part:] = jnp.where(first, got[i, :, extra:], keep[i, :, extra:]).astype(F32)


def run(kernel, name, place, local, remote, outs, far_outs, scratch, flops):
    vmem, anywhere = pl.BlockSpec(memory_space=pltpu.VMEM), pl.BlockSpec(memory_space=pl.ANY)
    shapes = [jax.ShapeDtypeStruct(*o) for o in tuple(outs) + tuple(far_outs)]
    size = sum(a.size * a.dtype.itemsize for a in (*local, *remote))
    size += sum(a.size * a.dtype.itemsize for a in shapes)
    return pl.pallas_call(
        kernel,
        out_shape=shapes,
        in_specs=[pl.BlockSpec(memory_space=pltpu.SMEM)]
        + [vmem] * len(local)
        + [anywhere] * len(remote),
        out_specs=[vmem] * len(outs) + [anywhere] * len(far_outs),
        scratch_shapes=scratch,
        compiler_params=pltpu.CompilerParams(vmem_limit_bytes=44 << 20),
        cost_estimate=pl.CostEstimate(
            flops=flops, bytes_accessed=size, transcendentals=0
        ),
        name=name,
    )(place, *local, *remote)


def on_device(tokens, expert_ids, gate_vals, w_gate, w_up, w_down, cotangent):
    core = lax.axis_index("expert") % 2
    y, x = lax.axis_index("fsdp") // 4, lax.axis_index("fsdp") % 4
    side, low = x // 2, x % 2
    rows, width = w_gate.shape[1:]
    depth = tokens.shape[1]
    part = half_width(width)
    quarter = 4 * MOST
    count = 4 * quarter
    work = count * depth * part * 2
    dma, row_dma = pltpu.SemaphoreType.DMA((13,)), pltpu.SemaphoreType.DMA((16,))
    row_scratch = pltpu.VMEM((count, depth), BF16)
    place = jnp.stack([y, side, low, core]).astype(jnp.int32)
    ids, gates = expert_ids.T, gate_vals.T
    r = Rounds()
    send = r.send

    def join(*arrays):
        return jnp.concatenate(arrays, axis=0)

    slices = ((3, rows, part), BF16)
    keep, give = run(
        split_kernel,
        "split",
        place,
        (),
        (w_gate, w_up, w_down),
        [slices] * 2,
        [],
        [pltpu.VMEM((3, rows, width), BF16), pltpu.SemaphoreType.DMA((3,))],
        1,
    )
    got = send("core", give)
    own_gu, own_dn, away_gu, away_dn = run(
        choose_kernel,
        "choose",
        place,
        (keep, got),
        (),
        [((2, rows, part), BF16), ((1, rows, part), BF16)] * 2,
        [],
        [],
        1,
    )
    r.next()
    side_gu = send("side", own_gu)
    mir0 = send("mirror", away_gu)
    own3 = send("up", own_dn)
    own1 = send("down", own_dn)
    r.next()
    block0 = in_pair(low == 0, own_gu, side_gu, 1)
    mir3 = send("up", mir0)
    mir1 = send("down", mir0)
    dn_mir = send("mirror", away_dn)
    both, oth, goth = dispatch(r.late(place), ids, gates, tokens, cotangent)
    home = r.exchange(r.late(both).reshape(4, 2 * MOST, depth), 2)
    r.next()
    block3 = send("up", block0)
    far = send("down", join(mir1, own1))
    side_a = send("side", join(mir0, mir1, dn_mir))
    tok_mir = send("mirror", oth)
    r.next()
    block_dn = in_pair(low == 1, dn_mir, side_a[4:], 1)
    block2 = send("up", block3)
    block1 = send("down", block0)
    side_b = send("side", join(mir3, far))
    grad_mir = send("mirror", goth)
    home_got = r.hold(lax.ppermute(r.late(home), AXES, TO_CORE))
    seen_tok = r.exchange(tok_mir.reshape(4, MOST, depth), 2)
    r.next()
    dn3 = send("up", block_dn)
    dn1 = send("down", block_dn)
    own_side = send("side", join(own_dn, own1, own3))
    tok_got = r.hold(lax.ppermute(after(seen_tok, side_b), AXES, TO_CORE))
    token_rows = (home, seen_tok, home_got, tok_got)
    gu_pieces = (block0, block1, block2, block3, mir0, mir1, mir3, far, side_a, side_b)
    hidden, fa, fb = run(
        forward_kernel,
        "forward",
        r.late(place),
        (),
        token_rows + gu_pieces,
        [((count, part), BF16), ((count, part), F32), ((count, part), F32)],
        [],
        [row_scratch, pltpu.VMEM((2, depth, part), BF16), dma, row_dma],
        2 * work,
    )
    r.hold(hidden)
    seen_grad = r.exchange(r.late(grad_mir).reshape(4, MOST, depth))
    r.next()
    dn2a = send("up", r.pin(dn3)[:, :rows])
    dn2b = send("down", r.pin(dn1)[:, rows:])
    grad_got = r.hold(lax.ppermute(r.pin(seen_grad), AXES, TO_CORE))
    grad_rows = (home, seen_grad, home_got, grad_got)
    own_keep, own_give, mir_t0, mir_t1, mir_t2, mir_t3 = run(
        down_term_kernel,
        "down_term",
        place,
        (r.pin(hidden),),
        grad_rows,
        [],
        [((4, rows, part), BF16)] * 2 + [((1, 2 * rows, part), BF16)] * 4,
        [row_scratch, pltpu.VMEM((depth, part), BF16), row_dma, dma],
        work,
    )
    r.hold(own_give)
    r.next()
    dn_pieces = (own_dn, own1, own3, far, own_side, side_b, block_dn, dn1, dn2a, dn2b, dn3)
    dn_far = send("down", mir_t2)
    dn_back = send("up", mir_t1)
    own_got = send("side", own_give)
    hidden_grads, blk_t0, blk_t1, blk_t2, blk_t3, mir_keep, give_a, give_b = run(
        gradient_kernel,
        "gradient",
        place,
        (r.pin(fa), fb),
        grad_rows + token_rows + dn_pieces,
        [((2, count, part), BF16)],
        [((2, 2 * rows, part), BF16)] * 4
        + [((4, 2, rows, part), BF16)]
        + [((2, 2, rows, part), BF16)] * 2,
        [row_scratch, row_scratch]
        + [pltpu.VMEM((depth, part), BF16), pltpu.VMEM((2, depth, part), BF16)]
        + [dma, dma, row_dma, row_dma],
        3 * work,
    )
    r.hold(give_a)

    r.next()
    own_sum = add(own_keep, own_got)
    blk_far = send("up", blk_t2)
    blk_back = send("down", blk_t3)
    got_a = send("side", give_a)
    own_far = send("down", own_sum[2:3])
    out_mine, grad_mine, theirs = run(
        output_kernel,
        "outputs",
        place,
        (r.pin(hidden), hidden_grads),
        gu_pieces + dn_pieces,
        [((count // 2, depth), F32)] * 2 + [((count, depth), BF16)],
        [],
        [pltpu.VMEM((2, depth, part), BF16), pltpu.VMEM((depth, part), BF16), dma, dma],
        3 * work,
    )
    r.hold(theirs)
    r.next()
    two, three = ((2, rows, part), BF16), ((3, rows, part), BF16)
    blk_mid, mir_mid, dn_mid = run(
        near_kernel,
        "near",
        place,
        (r.pin(blk_far), blk_t1, mir_keep, got_a, dn_far, mir_t3, own_far, own_sum),
        (),
        [((2, 2 * rows, part), BF16), two, ((1, 3 * rows, part), BF16)],
        [],
        [],
        1,
    )
    blk_near = send("up", blk_mid)
    mir_far = send("down", mir_mid)
    got_b = send("side", give_b)
    dn_down = send("down", dn_mid)
    got = send("core", theirs)
    out = r.hold(add(r.late(out_mine), got[: 2 * quarter]))
    out_home = r.exchange(out[quarter:].reshape(4, MOST, depth))
    grd = r.hold(add(r.late(grad_mine), got[2 * quarter :]))
    grad_home = r.exchange(grd[quarter:].reshape(4, MOST, depth), 2)
    r.next()
    stay, leave, up_sum, down_sum = run(
        cross_kernel,
        "cross",
        place,
        (blk_t0, blk_back, r.pin(blk_near), mir_t0, dn_back, r.pin(dn_down), mir_keep)
        + (got_a, got_b, mir_far, own_sum),
        (),
        [three, three, three, two],
        [],
        [],
        1,
    )
    mir_back = send("up", up_sum)
    mir_near = send("down", down_sum)
    leave_got = send("side", leave)
    out_oth = send("mirror", out_home.reshape(quarter, depth))
    out_own = r.exchange(r.late(out[:quarter]).reshape(4, MOST, depth), 2)
    r.next()
    mir_sum, own = run(
        last_kernel,
        "last",
        place,
        (stay, r.pin(leave_got), mir_keep, got_b, r.pin(mir_back), mir_near, own_sum, dn_down),
        (),
        [three, three],
        [],
        [],
        1,
    )
    away = send("mirror", mir_sum)
    grad_oth = send("mirror", grad_home.reshape(quarter, depth))
    grad_own = r.exchange(r.late(grd[:quarter]).reshape(4, MOST, depth))
    out_own, grad_own = out_own.reshape(quarter, depth), grad_own.reshape(quarter, depth)
    kept, give = run(pick_kernel, "pick", place, (own, away), (), [three, three], [], [], 1)
    other = lax.ppermute(give, AXES, TO_CORE)
    wide = ((1, rows, width), F32)
    grad_gate, grad_up, grad_down = run(
        widen_kernel, "widen", place, (kept, other), (), [wide] * 3, [], [], 1
    )

    output, grad_tokens, grad_gates = combine(
        place, ids, gates, cotangent, out_own, out_oth, grad_own, grad_oth
    )
    return (output, grad_tokens, grad_gates.T, grad_gate, grad_up, grad_down)


def solution(mesh):
    rows, weight = P(AXES, None), P("expert", "fsdp", None)
    return jax.shard_map(
        on_device,
        mesh=mesh,
        in_specs=(rows, rows, rows, weight, weight, weight, rows),
        out_specs=(rows, rows, rows, weight, weight, weight),
        check_vma=False,
    )
```

```python
import functools

import jax
import jax.numpy as jnp
from jax import lax
from jax.experimental import pallas as pl
from jax.experimental.pallas import tpu as pltpu
from jax.sharding import PartitionSpec as P

TOP = 6
MOST = 48
OWNED = 8
LANE = 128
AXES = ("expert", "fsdp")
F32 = jnp.float32
BF16 = jnp.bfloat16


def pairs_of(move):
    pairs = []
    for source in range(128):
        z, core, y, x = source // 32, source // 16 % 2, source // 4 % 4, source % 4
        core, y, x = move(core, y, x)
        pairs.append((source, (z * 2 + core) * 16 + y % 4 * 4 + x))
    return pairs


TO_CORE = pairs_of(lambda core, y, x: (1 - core, y, x))
TO_MIRROR = pairs_of(lambda core, y, x: (core, y, 3 - x))
TO_SIDE = pairs_of(lambda core, y, x: (core, y, x ^ 1))
TO_UP = pairs_of(lambda core, y, x: (core, y + 1, x))
TO_DOWN = pairs_of(lambda core, y, x: (core, y - 1, x))
Z_GROUPS = [[0, 2, 4, 6], [1, 3, 5, 7]]


MOVES = {"core": TO_CORE, "mirror": TO_MIRROR, "side": TO_SIDE, "up": TO_UP, "down": TO_DOWN, "rows": TO_MIRROR}


def after(value, *others):
    return lax.optimization_barrier((value,) + others)[0]


class Rounds:
    def __init__(self):
        self.number, self.held, self.ended, self.ready = 0, [], (), []

    def hold(self, value, rounds=1):
        self.held.append((self.number + rounds, value))
        return value

    def pin(self, value):
        return after(value, *self.ended) if self.ended else value

    def late(self, value):
        return after(value, *self.ready)

    def send(self, link, value, rounds=1):
        value = self.pin(value)
        self.ready.append(value)
        return self.hold(lax.ppermute(value, AXES, MOVES[link]), rounds)

    def exchange(self, value, rounds=1):
        moved = lax.all_to_all(
            value,
            "expert",
            split_axis=0,
            concat_axis=0,
            tiled=True,
            axis_index_groups=Z_GROUPS,
        )
        return self.hold(moved, rounds)

    def next(self):
        self.number += 1
        self.ready = []
        self.ended = tuple(v for due, v in self.held if due == self.number)


def routes(ids, half, own):
    tok_count = ids.shape[1]
    side = half if own else 1 - half
    live = []
    for z in range(4):
        wanted = OWNED * (2 * z + side)
        live.append(jnp.sum(jnp.where(ids == wanted, 1.0, 0.0), axis=0, keepdims=True))
    live = jnp.concatenate(live + [jnp.zeros((4, tok_count), F32)], axis=0)
    before = lax.broadcasted_iota(jnp.int32, (tok_count, tok_count), 0)
    after = lax.broadcasted_iota(jnp.int32, (tok_count, tok_count), 1)
    earlier = jnp.where(before < after, 1.0, 0.0).astype(BF16)
    rank = jnp.dot(live.astype(BF16), earlier, preferred_element_type=F32)
    row = lax.broadcasted_iota(jnp.int32, (MOST, tok_count), 0).astype(F32)
    chosen = []
    for z in range(4):
        here = jnp.where(row == rank[z : z + 1], 1.0, 0.0) * live[z : z + 1]
        chosen.append(here)
    return chosen


def gates_of(ids, gates, half, own):
    side = half if own else 1 - half
    return [
        jnp.sum(jnp.where(ids == OWNED * (2 * z + side), gates, 0.0), axis=0, keepdims=True)
        for z in range(4)
    ]


def dispatch_kernel(place, ids_ref, gates_ref, tok_ref, cot_ref, *outs):
    y, half = place[0], place[1]
    ids = ids_ref[...]
    gates = gates_ref[...].astype(F32)
    width = tok_ref.shape[1] // 8
    for own in (True, False):
        chosen = routes(ids, half, own)
        gate = gates_of(ids, gates, half, own)
        weight = jnp.concatenate(
            [jnp.sum(s * g, axis=1, keepdims=True) for s, g in zip(chosen, gate)], axis=0
        )
        select = jnp.concatenate(chosen, axis=0).astype(BF16)
        side = half if own else 1 - half
        for kind in range(2):
            for step in range(4):
                block = lax.rem(y + step, 4) * 2 + (side if kind == 0 else 1 - side)
                read = pl.ds(pl.multiple_of(block * width, width), width)
                put = slice((kind * 4 + step) * width, (kind * 4 + step + 1) * width)
                rows = jnp.dot(select, tok_ref[:, read], preferred_element_type=F32).astype(BF16)
                cots = jnp.dot(select, cot_ref[:, read], preferred_element_type=F32)
                grads = (weight * cots).astype(BF16)
                if own:
                    for z in range(4):
                        at, part = 2 * z * MOST, slice(z * MOST, (z + 1) * MOST)
                        outs[0][at : at + MOST, put] = rows[part]
                        outs[0][at + MOST : at + 2 * MOST, put] = grads[part]
                else:
                    outs[1][:, put] = rows
                    outs[2][:, put] = grads


def dispatch(place, ids, gates, tokens, cotangent):
    width = tokens.shape[1]
    both = jax.ShapeDtypeStruct((8 * MOST, width), BF16)
    rows = jax.ShapeDtypeStruct((4 * MOST, width), BF16)
    whole = pl.BlockSpec(memory_space=pltpu.VMEM)
    return pl.pallas_call(
        dispatch_kernel,
        out_shape=(both, rows, rows),
        in_specs=[pl.BlockSpec(memory_space=pltpu.SMEM)] + [whole] * 4,
        out_specs=(whole,) * 3,
        compiler_params=pltpu.CompilerParams(vmem_limit_bytes=48 << 20),
        cost_estimate=pl.CostEstimate(
            flops=1_000_000_000, bytes_accessed=6_000_000, transcendentals=0
        ),
        name="dispatch",
    )(place, ids, gates, tokens, cotangent)


TURNED = (((0,), (0,)), ((), ()))


def combine_kernel(
    place, ids_ref, gates_ref, cot_ref, own_ref, oth_ref, gown_ref, goth_ref, out_ref, gtok_ref, gg_ref
):
    y, half = place[0], place[1]
    ids = ids_ref[...]
    gates = gates_ref[...].astype(F32)
    width = cot_ref.shape[1] // 8
    picked, weighted, chosen_of = [], [], []
    for own in (True, False):
        chosen = routes(ids, half, own)
        gate = gates_of(ids, gates, half, own)
        picked.append(jnp.concatenate(chosen, axis=0).astype(BF16))
        weighted.append(
            jnp.concatenate([s * g for s, g in zip(chosen, gate)], axis=0).astype(BF16)
        )
        chosen_of.append(chosen)
    totals = [jnp.zeros((4 * MOST, 1), F32) for _ in range(2)]
    for step in range(4):
        for kind in range(2):
            block = lax.rem(y + step, 4) * 2 + (half if kind == 0 else 1 - half)
            at = pl.ds(pl.multiple_of(block * width, width), width)
            mine = slice((kind * 4 + step) * width, (kind * 4 + step + 1) * width)
            other = slice(((1 - kind) * 4 + step) * width, ((1 - kind) * 4 + step + 1) * width)
            cot = cot_ref[:, at]
            outs = (own_ref[:, mine], oth_ref[:, other])
            grads = (gown_ref[:, mine], goth_ref[:, other])
            out_ref[:, at] = sum(
                lax.dot_general(w, o, TURNED, preferred_element_type=F32)
                for w, o in zip(weighted, outs)
            ).astype(BF16)
            gtok_ref[:, at] = sum(
                lax.dot_general(s, g, TURNED, preferred_element_type=F32)
                for s, g in zip(picked, grads)
            ).astype(BF16)
            for i in range(2):
                cots = jnp.dot(picked[i], cot, preferred_element_type=F32)
                totals[i] += jnp.sum(cots * outs[i].astype(F32), axis=1, keepdims=True)
    result = jnp.zeros(ids.shape, F32)
    for i, own in enumerate((True, False)):
        side = half if own else 1 - half
        for z in range(4):
            per_slot = totals[i][z * MOST : (z + 1) * MOST]
            per_token = jnp.sum(chosen_of[i][z] * per_slot, axis=0, keepdims=True)
            result += jnp.where(ids == OWNED * (2 * z + side), per_token, 0.0)
    gg_ref[...] = result


def combine(place, ids, gates, cotangent, own, oth, gown, goth):
    shape = jax.ShapeDtypeStruct(cotangent.shape, BF16)
    whole = pl.BlockSpec(memory_space=pltpu.VMEM)
    return pl.pallas_call(
        combine_kernel,
        out_shape=(shape, shape, jax.ShapeDtypeStruct(ids.shape, F32)),
        in_specs=[pl.BlockSpec(memory_space=pltpu.SMEM)] + [whole] * 7,
        out_specs=(whole,) * 3,
        compiler_params=pltpu.CompilerParams(vmem_limit_bytes=48 << 20),
        cost_estimate=pl.CostEstimate(
            flops=2_000_000_000, bytes_accessed=8_000_000, transcendentals=0
        ),
        name="combine",
    )(place, ids, gates, cotangent, own, oth, gown, goth)


def half_width(width):
    return -(-width // (2 * LANE)) * LANE


def split_kernel(place, gate_hbm, up_hbm, down_hbm, keep_ref, give_ref, refs, sems):
    hbms = (gate_hbm, up_hbm, down_hbm)
    started = fetch([(hbm.at[0], refs.at[i]) for i, hbm in enumerate(hbms)], sems)
    part = keep_ref.shape[2]
    width = refs.shape[2]
    first = place[3] == 0
    for i, copy in enumerate(started):
        copy.wait()
        left = refs[i, :, :part]
        blank = jnp.zeros((left.shape[0], 2 * part - width), left.dtype)
        right = jnp.concatenate([blank, refs[i, :, part:]], axis=1)
        keep_ref[i] = jnp.where(first, left, right)
        give_ref[i] = jnp.where(first, right, left)


def choose_kernel(place, keep_ref, got_ref, own_gu, own_dn, away_gu, away_dn):
    here = place[3] == place[1]
    for i in range(3):
        own, away, at = (own_gu, away_gu, i) if i < 2 else (own_dn, away_dn, 0)
        own[at] = jnp.where(here, keep_ref[i], got_ref[i])
        away[at] = jnp.where(here, got_ref[i], keep_ref[i])


def in_pair(first, mine, theirs, axis):
    return jnp.where(
        first,
        jnp.concatenate([mine, theirs], axis=axis),
        jnp.concatenate([theirs, mine], axis=axis),
    )


def add(*terms):
    return sum(t.astype(F32) for t in terms).astype(BF16)


def dot(a, b, over):
    return lax.dot_general(a, b, (over, ((), ())), preferred_element_type=F32)


WIDE = 256


def fetch(copies, sems):
    started = [pltpu.make_async_copy(a, b, sems.at[i]) for i, (a, b) in enumerate(copies)]
    for copy in started:
        copy.start()
    return started


def gate_up_pieces(low, refs, full):
    block0, block1, block2, block3, mir0, mir1, mir3, far, side_a, side_b = refs
    rows = mir0.shape[1]
    copies = [
        (block, full.at[:, pl.ds(2 * rows * i, 2 * rows), :])
        for i, block in enumerate((block0, block1, block2, block3))
    ]
    for i, (mine, theirs) in enumerate(
        (
            (mir0, side_a.at[0:2]),
            (mir1, side_a.at[2:4]),
            (far.at[0:2], side_b.at[2:4]),
            (mir3, side_b.at[0:2]),
        )
    ):
        start = (8 + 2 * i) * rows
        copies.append((mine, full.at[:, pl.ds(start + (1 - low) * rows, rows), :]))
        copies.append((theirs, full.at[:, pl.ds(start + low * rows, rows), :]))
    return copies


def down_pieces(low, refs, full):
    own0, own1, own3, far, side, side_b, block0, block1, block2a, block2b, block3 = refs
    rows = own0.shape[1]
    copies = []
    for i, (mine, theirs) in enumerate(
        (
            (own0.at[0], side.at[0]),
            (own1.at[0], side.at[1]),
            (far.at[2], side_b.at[4]),
            (own3.at[0], side.at[2]),
        )
    ):
        start = 2 * rows * i
        copies.append((mine, full.at[pl.ds(start + low * rows, rows), :]))
        copies.append((theirs, full.at[pl.ds(start + (1 - low) * rows, rows), :]))
    for at, size, block in (
        (8, 2, block0),
        (10, 2, block1),
        (12, 1, block2a),
        (13, 1, block2b),
        (14, 2, block3),
    ):
        copies.append((block.at[0], full.at[pl.ds(at * rows, size * rows), :]))
    return copies


def chunk(i, size=WIDE):
    return pl.ds(pl.multiple_of(i * size, size), size)


def row_pieces(refs, first, full):
    copies = []
    for core, (home, seen) in enumerate((refs[:2], refs[2:])):
        for z in range(4):
            at = (core * 8 + z) * MOST
            copies.append((home.at[z, pl.ds(first, MOST)], full.at[pl.ds(at, MOST)]))
            copies.append((seen.at[z], full.at[pl.ds(at + 4 * MOST, MOST)]))
    return copies


def forward_kernel(place, *refs):
    row_refs, pieces, (hid_ref, fa_ref, fb_ref, rows_ref, full, sems, row_sems) = (
        refs[:4],
        refs[4:14],
        refs[14:],
    )
    started = fetch(row_pieces(row_refs, 0, rows_ref), row_sems)
    started += fetch(gate_up_pieces(place[2], pieces, full), sems)
    for copy in started:
        copy.wait()

    def step(i, unused):
        gate = dot(rows_ref[...], full[0, :, chunk(i)], ((1,), (0,)))
        up = dot(rows_ref[...], full[1, :, chunk(i)], ((1,), (0,)))
        sig = 1.0 / (1.0 + jnp.exp(-gate))
        silu = gate * sig
        hid_ref[:, chunk(i)] = (silu * up).astype(BF16)
        fa_ref[:, chunk(i)] = up * sig * (1.0 + gate * (1.0 - sig))
        fb_ref[:, chunk(i)] = silu
        return unused

    lax.fori_loop(0, hid_ref.shape[1] // WIDE, step, 0)


def term_of(at, rows_ref, right_ref):
    return dot(rows_ref[:, at], right_ref[...], ((0,), (0,))).astype(BF16)


def down_term_kernel(place, hid_ref, *refs):
    row_refs, (keep, give, mir0, mir1, mir2, mir3) = refs[:4], refs[4:10]
    rows_ref, terms, row_sems, sems = refs[10:]
    for copy in fetch(row_pieces(row_refs, MOST, rows_ref), row_sems):
        copy.wait()
    low = place[2]
    rows = keep.shape[1]
    half = terms.shape[0] // 2
    owns, mirs = [], []
    for i in range(4):
        start = 2 * rows * i
        owns.append((terms.at[pl.ds(start + low * rows, rows), :], keep.at[i]))
        owns.append((terms.at[pl.ds(start + (1 - low) * rows, rows), :], give.at[i]))
    for i, mir in enumerate((mir0, mir1, mir2, mir3)):
        mirs.append((terms.at[pl.ds(half + 2 * i * rows, 2 * rows), :], mir.at[0]))
    terms[:half, :] = term_of(slice(0, half), rows_ref, hid_ref)
    started = fetch(owns, sems)
    terms[half:, :] = term_of(slice(half, 2 * half), rows_ref, hid_ref)
    started += fetch(mirs, row_sems)
    for copy in started:
        copy.wait()


def gradient_kernel(place, fa_ref, fb_ref, *refs):
    grad_refs, tok_refs, pieces, refs = refs[:4], refs[4:8], refs[8:19], refs[19:]
    both_ref, blk0, blk1, blk2, blk3, keep, give_a, give_b = refs[:8]
    g_rows, x_rows, full, terms, in_sems, out_sems, g_sems, x_sems = refs[8:]
    low = place[2]
    rows = give_b.shape[2]
    started = fetch(row_pieces(grad_refs, MOST, g_rows), g_sems)
    started += fetch(down_pieces(low, pieces, full), in_sems)
    later = fetch(row_pieces(tok_refs, 0, x_rows), x_sems)
    for copy in started:
        copy.wait()

    def step(i, unused):
        hidden_grad = dot(g_rows[...], full[:, chunk(i)], ((1,), (0,)))
        both_ref[0, :, chunk(i)] = (hidden_grad * fa_ref[:, chunk(i)]).astype(BF16)
        both_ref[1, :, chunk(i)] = (hidden_grad * fb_ref[:, chunk(i)]).astype(BF16)
        return unused

    lax.fori_loop(0, both_ref.shape[2] // WIDE, step, 0)
    for copy in later:
        copy.wait()

    half = terms.shape[1] // 2
    blocks, mirs = [], []
    for i, blk in enumerate((blk0, blk1, blk2, blk3)):
        blocks.append((terms.at[:, pl.ds(2 * rows * i, 2 * rows), :], blk))
    for i, give in enumerate((give_b.at[0], give_a.at[1], give_a.at[0], give_b.at[1])):
        start = (8 + 2 * i) * rows
        mirs.append((terms.at[:, pl.ds(start + (1 - low) * rows, rows), :], keep.at[i]))
        mirs.append((terms.at[:, pl.ds(start + low * rows, rows), :], give))
    started = []
    for copies, first, sems in ((blocks, 0, in_sems), (mirs, half, out_sems)):
        at = slice(first, first + half)

        def put(i, unused, at=at):
            terms[i, at, :] = dot(x_rows[:, at], both_ref[i], ((0,), (0,))).astype(BF16)
            return unused

        lax.fori_loop(0, 2, put, 0)
        started += fetch(copies, sems)
    for copy in started:
        copy.wait()


def output_kernel(place, hid_ref, both_ref, *refs):
    up_pieces, dn_pieces, refs = refs[:10], refs[10:21], refs[21:]
    out_mine, grad_mine, theirs, full, down, sems, down_sems = refs
    low = place[2]
    first = fetch(down_pieces(low, dn_pieces, down), down_sems)
    second = fetch(gate_up_pieces(low, up_pieces, full), sems)
    count = out_mine.shape[0]
    for copy in first:
        copy.wait()

    half = down.shape[0] // 2

    def out_step(i, unused):
        at = chunk(i, half)
        out_mine[:, at] = dot(hid_ref[:count, :], down[at, :], ((1,), (1,)))
        theirs[:count, at] = dot(hid_ref[count:, :], down[at, :], ((1,), (1,))).astype(BF16)
        return unused

    lax.fori_loop(0, 2, out_step, 0)
    for copy in second:
        copy.wait()

    def grad_step(i, unused):
        at = chunk(i, half)
        gate, up = full[0, at, :], full[1, at, :]
        for mine, to in ((slice(0, count), grad_mine), (slice(count, 2 * count), theirs)):
            total = dot(both_ref[0, mine, :], gate, ((1,), (1,))) + dot(
                both_ref[1, mine, :], up, ((1,), (1,))
            )
            to[mine if to is theirs else slice(None), at] = total.astype(to.dtype)
        return unused

    lax.fori_loop(0, 2, grad_step, 0)


STEP = 64


def sum_rows(to, *terms):
    def step(i, unused):
        at = chunk(i, STEP)
        to[at, :] = sum(t[at, :].astype(F32) for t in terms).astype(to.dtype)
        return unused

    lax.fori_loop(0, to.shape[0] // STEP, step, 0)


def near_kernel(place, blk_far, blk1, keep, got_a, dn_far, mir3, own_far, own_sum, blk, both):
    rows = both.shape[1]
    for g in range(2):
        sum_rows(blk.at[g], blk_far.at[g], blk1.at[g])
        sum_rows(both.at[g], keep.at[2, g], got_a.at[0, g])
        at = slice(g * rows, (g + 1) * rows)
        sum_rows(both.at[2 + g], dn_far.at[0, at], mir3.at[0, at])
    sum_rows(both.at[4], own_far.at[0], own_sum.at[3])


def widen_kernel(place, keep, got, *outs):
    first = place[3] == 0
    part = keep.shape[2]
    for i, out in enumerate(outs):
        extra = 2 * part - out.shape[2]
        out[0, :, :part] = jnp.where(first, keep[i], got[i]).astype(F32)
        out[0, :, part:] = jnp.where(first, got[i, :, extra:], keep[i, :, extra:]).astype(F32)


def run(kernel, name, place, local, remote, outs, far_outs, scratch, flops):
    vmem, anywhere = pl.BlockSpec(memory_space=pltpu.VMEM), pl.BlockSpec(memory_space=pl.ANY)
    shapes = [jax.ShapeDtypeStruct(*o) for o in tuple(outs) + tuple(far_outs)]
    size = sum(a.size * a.dtype.itemsize for a in (*local, *remote))
    size += sum(a.size * a.dtype.itemsize for a in shapes)
    return pl.pallas_call(
        kernel,
        out_shape=shapes,
        in_specs=[pl.BlockSpec(memory_space=pltpu.SMEM)]
        + [vmem] * len(local)
        + [anywhere] * len(remote),
        out_specs=[vmem] * len(outs) + [anywhere] * len(far_outs),
        scratch_shapes=scratch,
        compiler_params=pltpu.CompilerParams(vmem_limit_bytes=44 << 20),
        cost_estimate=pl.CostEstimate(
            flops=flops, bytes_accessed=size, transcendentals=0
        ),
        name=name,
    )(place, *local, *remote)


def on_device(tokens, expert_ids, gate_vals, w_gate, w_up, w_down, cotangent):
    core = lax.axis_index("expert") % 2
    y, x = lax.axis_index("fsdp") // 4, lax.axis_index("fsdp") % 4
    side, low = x // 2, x % 2
    rows, width = w_gate.shape[1:]
    depth = tokens.shape[1]
    part = half_width(width)
    quarter = 4 * MOST
    count = 4 * quarter
    work = count * depth * part * 2
    dma, row_dma = pltpu.SemaphoreType.DMA((13,)), pltpu.SemaphoreType.DMA((16,))
    row_scratch = pltpu.VMEM((count, depth), BF16)
    place = jnp.stack([y, side, low, core]).astype(jnp.int32)
    ids, gates = expert_ids.T, gate_vals.T
    r = Rounds()
    send = r.send

    def join(*arrays):
        return jnp.concatenate(arrays, axis=0)

    slices = ((3, rows, part), BF16)
    keep, give = run(
        split_kernel,
        "split",
        place,
        (),
        (w_gate, w_up, w_down),
        [slices] * 2,
        [],
        [pltpu.VMEM((3, rows, width), BF16), pltpu.SemaphoreType.DMA((3,))],
        1,
    )
    got = send("core", give)
    own_gu, own_dn, away_gu, away_dn = run(
        choose_kernel,
        "choose",
        place,
        (keep, got),
        (),
        [((2, rows, part), BF16), ((1, rows, part), BF16)] * 2,
        [],
        [],
        1,
    )
    r.next()
    side_gu = send("side", own_gu)
    mir0 = send("mirror", away_gu)
    own3 = send("up", own_dn)
    own1 = send("down", own_dn)
    r.next()
    block0 = in_pair(low == 0, own_gu, side_gu, 1)
    mir3 = send("up", mir0)
    mir1 = send("down", mir0)
    dn_mir = send("mirror", away_dn)
    both, oth, goth = dispatch(r.late(place), ids, gates, tokens, cotangent)
    home = r.exchange(r.late(both).reshape(4, 2 * MOST, depth), 2)
    r.next()
    block3 = send("up", block0)
    far = send("down", join(mir1, own1))
    side_a = send("side", join(mir0, mir1, dn_mir))
    tok_mir = send("mirror", oth)
    r.next()
    block_dn = in_pair(low == 1, dn_mir, side_a[4:], 1)
    block2 = send("up", block3)
    block1 = send("down", block0)
    side_b = send("side", join(mir3, far))
    grad_mir = send("mirror", goth)
    home_got = r.hold(lax.ppermute(r.late(home), AXES, TO_CORE))
    seen_tok = r.exchange(tok_mir.reshape(4, MOST, depth), 2)
    r.next()
    dn3 = send("up", block_dn)
    dn1 = send("down", block_dn)
    own_side = send("side", join(own_dn, own1, own3))
    tok_got = r.hold(lax.ppermute(after(seen_tok, side_b), AXES, TO_CORE))
    token_rows = (home, seen_tok, home_got, tok_got)
    gu_pieces = (block0, block1, block2, block3, mir0, mir1, mir3, far, side_a, side_b)
    hidden, fa, fb = run(
        forward_kernel,
        "forward",
        r.late(place),
        (),
        token_rows + gu_pieces,
        [((count, part), BF16), ((count, part), F32), ((count, part), F32)],
        [],
        [row_scratch, pltpu.VMEM((2, depth, part), BF16), dma, row_dma],
        2 * work,
    )
    r.hold(hidden)
    seen_grad = r.exchange(r.late(grad_mir).reshape(4, MOST, depth))
    r.next()
    dn2a = send("up", r.pin(dn3)[:, :rows])
    dn2b = send("down", r.pin(dn1)[:, rows:])
    grad_got = r.hold(lax.ppermute(r.pin(seen_grad), AXES, TO_CORE))
    grad_rows = (home, seen_grad, home_got, grad_got)
    own_keep, own_give, mir_t0, mir_t1, mir_t2, mir_t3 = run(
        down_term_kernel,
        "down_term",
        place,
        (r.pin(hidden),),
        grad_rows,
        [],
        [((4, rows, part), BF16)] * 2 + [((1, 2 * rows, part), BF16)] * 4,
        [row_scratch, pltpu.VMEM((depth, part), BF16), row_dma, dma],
        work,
    )
    r.hold(own_give)
    r.next()
    dn_pieces = (own_dn, own1, own3, far, own_side, side_b, block_dn, dn1, dn2a, dn2b, dn3)
    dn_far = send("down", mir_t2)
    dn_back = send("up", mir_t1)
    own_got = send("side", own_give)
    hidden_grads, blk_t0, blk_t1, blk_t2, blk_t3, mir_keep, give_a, give_b = run(
        gradient_kernel,
        "gradient",
        place,
        (r.pin(fa), fb),
        grad_rows + token_rows + dn_pieces,
        [((2, count, part), BF16)],
        [((2, 2 * rows, part), BF16)] * 4
        + [((4, 2, rows, part), BF16)]
        + [((2, 2, rows, part), BF16)] * 2,
        [row_scratch, row_scratch]
        + [pltpu.VMEM((depth, part), BF16), pltpu.VMEM((2, depth, part), BF16)]
        + [dma, dma, row_dma, row_dma],
        3 * work,
    )
    r.hold(give_a)

    r.next()
    own_sum = add(own_keep, own_got)
    blk_far = send("up", blk_t2)
    blk_back = send("down", blk_t3)
    got_a = send("side", give_a)
    own_far = send("down", own_sum[2:3])
    out_mine, grad_mine, theirs = run(
        output_kernel,
        "outputs",
        place,
        (r.pin(hidden), hidden_grads),
        gu_pieces + dn_pieces,
        [((count // 2, depth), F32)] * 2 + [((count, depth), BF16)],
        [],
        [pltpu.VMEM((2, depth, part), BF16), pltpu.VMEM((depth, part), BF16), dma, dma],
        3 * work,
    )
    r.hold(theirs)
    r.next()
    blk_mid, both_mid = run(
        near_kernel,
        "near",
        place,
        (r.pin(blk_far), blk_t1, mir_keep, got_a, dn_far, mir_t3, own_far, own_sum),
        (),
        [((2, 2 * rows, part), BF16), ((5, rows, part), BF16)],
        [],
        [],
        1,
    )
    blk_near = send("up", blk_mid)
    got_b = send("side", give_b)
    both_far = send("down", both_mid)
    got = send("core", theirs)
    out = r.hold(add(r.late(out_mine), got[: 2 * quarter]))
    out_home = r.exchange(out[quarter:].reshape(4, MOST, depth))
    grd = r.hold(add(r.late(grad_mine), got[2 * quarter :]))
    grad_home = r.exchange(grd[quarter:].reshape(4, MOST, depth), 2)
    r.next()
    both_far, blk_near, blk_back = r.pin(both_far), r.pin(blk_near), r.pin(blk_back)
    mir_far, own_near = both_far[:2], both_far[4:]
    dn_near = both_far[2:4].reshape(1, 2 * rows, part)
    mir_back = send("up", jnp.concatenate([add(mir_keep[1], got_a[1]), own_sum[1:2]], axis=0))
    mir_near = send("down", add(mir_far, mir_keep[3], r.pin(got_b)[1]))
    blk = add(blk_t0, blk_back, blk_near)
    mir_dn = add(mir_t0, dn_back, dn_near)
    low_half, high_half = join(blk[:, :rows], mir_dn[:, rows:]), join(blk[:, rows:], mir_dn[:, :rows])
    stay = jnp.where(low == 0, low_half, high_half)
    leave_got = send("side", jnp.where(low == 0, high_half, low_half))
    out_oth = send("mirror", out_home.reshape(quarter, depth))
    out_own = r.exchange(r.late(out[:quarter]).reshape(4, MOST, depth), 2)
    r.next()
    here = core == side
    mir_back = r.pin(mir_back)
    mine = add(stay, r.pin(leave_got))
    gu_mir = add(mir_keep[0], got_b[0], mir_back[:2], r.pin(mir_near))
    away = send("mirror", join(gu_mir, mine[2:]))
    grad_oth = send("mirror", grad_home.reshape(quarter, depth))
    grad_own = r.exchange(r.late(grd[:quarter]).reshape(4, MOST, depth))
    out_own, grad_own = out_own.reshape(quarter, depth), grad_own.reshape(quarter, depth)
    own = join(mine[:2], add(own_sum[:1], mir_back[2:], own_near))
    other = lax.ppermute(jnp.where(here, away, own), AXES, TO_CORE)
    kept = jnp.where(here, own, away)
    wide = ((1, rows, width), F32)
    grad_gate, grad_up, grad_down = run(
        widen_kernel, "widen", place, (kept, other), (), [wide] * 3, [], [], 1
    )

    output, grad_tokens, grad_gates = combine(
        after(place, grad_down), ids, gates, cotangent, out_own, out_oth, grad_own, grad_oth
    )
    return (output, grad_tokens, grad_gates.T, grad_gate, grad_up, grad_down)


def solution(mesh):
    rows, weight = P(AXES, None), P("expert", "fsdp", None)
    return jax.shard_map(
        on_device,
        mesh=mesh,
        in_specs=(rows, rows, rows, weight, weight, weight, rows),
        out_specs=(rows, rows, rows, weight, weight, weight),
        check_vma=False,
    )
```

```python
import functools

import jax
import jax.numpy as jnp
from jax import lax
from jax.experimental import pallas as pl
from jax.experimental.pallas import tpu as pltpu
from jax.sharding import PartitionSpec as P

TOP = 6
MOST = 48
OWNED = 8
LANE = 128
AXES = ("expert", "fsdp")
F32 = jnp.float32
BF16 = jnp.bfloat16


def pairs_of(move):
    pairs = []
    for source in range(128):
        z, core, y, x = source // 32, source // 16 % 2, source // 4 % 4, source % 4
        core, y, x = move(core, y, x)
        pairs.append((source, (z * 2 + core) * 16 + y % 4 * 4 + x))
    return pairs


TO_CORE = pairs_of(lambda core, y, x: (1 - core, y, x))
TO_MIRROR = pairs_of(lambda core, y, x: (core, y, 3 - x))
TO_SIDE = pairs_of(lambda core, y, x: (core, y, x ^ 1))
TO_UP = pairs_of(lambda core, y, x: (core, y + 1, x))
TO_DOWN = pairs_of(lambda core, y, x: (core, y - 1, x))
Z_GROUPS = [[0, 2, 4, 6], [1, 3, 5, 7]]


MOVES = {"core": TO_CORE, "mirror": TO_MIRROR, "side": TO_SIDE, "up": TO_UP, "down": TO_DOWN, "rows": TO_MIRROR}


def after(value, *others):
    return lax.optimization_barrier((value,) + others)[0]


class Rounds:
    def __init__(self):
        self.number, self.held, self.ended, self.ready = 0, [], (), []

    def hold(self, value, rounds=1):
        self.held.append((self.number + rounds, value))
        return value

    def pin(self, value):
        return after(value, *self.ended) if self.ended else value

    def late(self, value):
        return after(value, *self.ready)

    def send(self, link, value, rounds=1):
        value = self.pin(value)
        self.ready.append(value)
        return self.hold(lax.ppermute(value, AXES, MOVES[link]), rounds)

    def exchange(self, value, rounds=1):
        moved = lax.all_to_all(
            value,
            "expert",
            split_axis=0,
            concat_axis=0,
            tiled=True,
            axis_index_groups=Z_GROUPS,
        )
        return self.hold(moved, rounds)

    def next(self):
        self.number += 1
        self.ready = []
        self.ended = tuple(v for due, v in self.held if due == self.number)


def routes(ids, half, own):
    tok_count = ids.shape[1]
    side = half if own else 1 - half
    live = []
    for z in range(4):
        wanted = OWNED * (2 * z + side)
        live.append(jnp.sum(jnp.where(ids == wanted, 1.0, 0.0), axis=0, keepdims=True))
    live = jnp.concatenate(live + [jnp.zeros((4, tok_count), F32)], axis=0)
    before = lax.broadcasted_iota(jnp.int32, (tok_count, tok_count), 0)
    after = lax.broadcasted_iota(jnp.int32, (tok_count, tok_count), 1)
    earlier = jnp.where(before < after, 1.0, 0.0).astype(BF16)
    rank = jnp.dot(live.astype(BF16), earlier, preferred_element_type=F32)
    row = lax.broadcasted_iota(jnp.int32, (MOST, tok_count), 0).astype(F32)
    chosen = []
    for z in range(4):
        here = jnp.where(row == rank[z : z + 1], 1.0, 0.0) * live[z : z + 1]
        chosen.append(here)
    return chosen


def gates_of(ids, gates, half, own):
    side = half if own else 1 - half
    return [
        jnp.sum(jnp.where(ids == OWNED * (2 * z + side), gates, 0.0), axis=0, keepdims=True)
        for z in range(4)
    ]


def dispatch_kernel(place, ids_ref, gates_ref, tok_ref, cot_ref, *outs):
    y, half = place[0], place[1]
    ids = ids_ref[...]
    gates = gates_ref[...].astype(F32)
    width = tok_ref.shape[1] // 8
    for own in (True, False):
        chosen = routes(ids, half, own)
        gate = gates_of(ids, gates, half, own)
        weight = jnp.concatenate(
            [jnp.sum(s * g, axis=1, keepdims=True) for s, g in zip(chosen, gate)], axis=0
        )
        select = jnp.concatenate(chosen, axis=0).astype(BF16)
        side = half if own else 1 - half
        for kind in range(2):
            for step in range(4):
                block = lax.rem(y + step, 4) * 2 + (side if kind == 0 else 1 - side)
                read = pl.ds(pl.multiple_of(block * width, width), width)
                put = slice((kind * 4 + step) * width, (kind * 4 + step + 1) * width)
                rows = jnp.dot(select, tok_ref[:, read], preferred_element_type=F32).astype(BF16)
                cots = jnp.dot(select, cot_ref[:, read], preferred_element_type=F32)
                grads = (weight * cots).astype(BF16)
                if own:
                    for z in range(4):
                        at, part = 2 * z * MOST, slice(z * MOST, (z + 1) * MOST)
                        outs[0][at : at + MOST, put] = rows[part]
                        outs[0][at + MOST : at + 2 * MOST, put] = grads[part]
                else:
                    outs[1][:, put] = rows
                    outs[2][:, put] = grads


def dispatch(place, ids, gates, tokens, cotangent):
    width = tokens.shape[1]
    both = jax.ShapeDtypeStruct((8 * MOST, width), BF16)
    rows = jax.ShapeDtypeStruct((4 * MOST, width), BF16)
    whole = pl.BlockSpec(memory_space=pltpu.VMEM)
    return pl.pallas_call(
        dispatch_kernel,
        out_shape=(both, rows, rows),
        in_specs=[pl.BlockSpec(memory_space=pltpu.SMEM)] + [whole] * 4,
        out_specs=(whole,) * 3,
        compiler_params=pltpu.CompilerParams(vmem_limit_bytes=48 << 20),
        cost_estimate=pl.CostEstimate(
            flops=1_000_000_000, bytes_accessed=6_000_000, transcendentals=0
        ),
        name="dispatch",
    )(place, ids, gates, tokens, cotangent)


TURNED = (((0,), (0,)), ((), ()))


def combine_kernel(
    place, ids_ref, gates_ref, cot_ref, own_ref, oth_ref, gown_ref, goth_ref, out_ref, gtok_ref, gg_ref
):
    y, half = place[0], place[1]
    ids = ids_ref[...]
    gates = gates_ref[...].astype(F32)
    width = cot_ref.shape[1] // 8
    picked, weighted, chosen_of = [], [], []
    for own in (True, False):
        chosen = routes(ids, half, own)
        gate = gates_of(ids, gates, half, own)
        picked.append(jnp.concatenate(chosen, axis=0).astype(BF16))
        weighted.append(
            jnp.concatenate([s * g for s, g in zip(chosen, gate)], axis=0).astype(BF16)
        )
        chosen_of.append(chosen)
    totals = [jnp.zeros((4 * MOST, 1), F32) for _ in range(2)]
    for step in range(4):
        for kind in range(2):
            block = lax.rem(y + step, 4) * 2 + (half if kind == 0 else 1 - half)
            at = pl.ds(pl.multiple_of(block * width, width), width)
            mine = slice((kind * 4 + step) * width, (kind * 4 + step + 1) * width)
            other = slice(((1 - kind) * 4 + step) * width, ((1 - kind) * 4 + step + 1) * width)
            cot = cot_ref[:, at]
            outs = (own_ref[:, mine], oth_ref[:, other])
            grads = (gown_ref[:, mine], goth_ref[:, other])
            out_ref[:, at] = sum(
                lax.dot_general(w, o, TURNED, preferred_element_type=F32)
                for w, o in zip(weighted, outs)
            ).astype(BF16)
            gtok_ref[:, at] = sum(
                lax.dot_general(s, g, TURNED, preferred_element_type=F32)
                for s, g in zip(picked, grads)
            ).astype(BF16)
            for i in range(2):
                cots = jnp.dot(picked[i], cot, preferred_element_type=F32)
                totals[i] += jnp.sum(cots * outs[i].astype(F32), axis=1, keepdims=True)
    result = jnp.zeros(ids.shape, F32)
    for i, own in enumerate((True, False)):
        side = half if own else 1 - half
        for z in range(4):
            per_slot = totals[i][z * MOST : (z + 1) * MOST]
            per_token = jnp.sum(chosen_of[i][z] * per_slot, axis=0, keepdims=True)
            result += jnp.where(ids == OWNED * (2 * z + side), per_token, 0.0)
    gg_ref[...] = result


def combine(place, ids, gates, cotangent, own, oth, gown, goth):
    shape = jax.ShapeDtypeStruct(cotangent.shape, BF16)
    whole = pl.BlockSpec(memory_space=pltpu.VMEM)
    return pl.pallas_call(
        combine_kernel,
        out_shape=(shape, shape, jax.ShapeDtypeStruct(ids.shape, F32)),
        in_specs=[pl.BlockSpec(memory_space=pltpu.SMEM)] + [whole] * 7,
        out_specs=(whole,) * 3,
        compiler_params=pltpu.CompilerParams(vmem_limit_bytes=48 << 20),
        cost_estimate=pl.CostEstimate(
            flops=2_000_000_000, bytes_accessed=8_000_000, transcendentals=0
        ),
        name="combine",
    )(place, ids, gates, cotangent, own, oth, gown, goth)


def half_width(width):
    return -(-width // (2 * LANE)) * LANE


def split_kernel(place, gate_hbm, up_hbm, down_hbm, keep_ref, give_ref, refs, sems):
    hbms = (gate_hbm, up_hbm, down_hbm)
    started = fetch([(hbm.at[0], refs.at[i]) for i, hbm in enumerate(hbms)], sems)
    part = keep_ref.shape[2]
    width = refs.shape[2]
    first = place[3] == 0
    for i, copy in enumerate(started):
        copy.wait()
        left = refs[i, :, :part]
        blank = jnp.zeros((left.shape[0], 2 * part - width), left.dtype)
        right = jnp.concatenate([blank, refs[i, :, part:]], axis=1)
        keep_ref[i] = jnp.where(first, left, right)
        give_ref[i] = jnp.where(first, right, left)


def choose_kernel(place, keep_ref, got_ref, own_gu, own_dn, away_gu, away_dn):
    here = place[3] == place[1]
    for i in range(3):
        own, away, at = (own_gu, away_gu, i) if i < 2 else (own_dn, away_dn, 0)
        own[at] = jnp.where(here, keep_ref[i], got_ref[i])
        away[at] = jnp.where(here, got_ref[i], keep_ref[i])


def in_pair(first, mine, theirs, axis):
    return jnp.where(
        first,
        jnp.concatenate([mine, theirs], axis=axis),
        jnp.concatenate([theirs, mine], axis=axis),
    )


def add(*terms):
    return sum(t.astype(F32) for t in terms).astype(BF16)


def dot(a, b, over):
    return lax.dot_general(a, b, (over, ((), ())), preferred_element_type=F32)


WIDE = 256


def fetch(copies, sems):
    started = [pltpu.make_async_copy(a, b, sems.at[i]) for i, (a, b) in enumerate(copies)]
    for copy in started:
        copy.start()
    return started


def gate_up_pieces(low, refs, full):
    block0, block1, block2, block3, mir0, mir1, mir3, far, side_a, side_b = refs
    rows = mir0.shape[1]
    copies = [
        (block, full.at[:, pl.ds(2 * rows * i, 2 * rows), :])
        for i, block in enumerate((block0, block1, block2, block3))
    ]
    for i, (mine, theirs) in enumerate(
        (
            (mir0, side_a.at[0:2]),
            (mir1, side_a.at[2:4]),
            (far.at[0:2], side_b.at[2:4]),
            (mir3, side_b.at[0:2]),
        )
    ):
        start = (8 + 2 * i) * rows
        copies.append((mine, full.at[:, pl.ds(start + (1 - low) * rows, rows), :]))
        copies.append((theirs, full.at[:, pl.ds(start + low * rows, rows), :]))
    return copies


def down_pieces(low, refs, full):
    own0, own1, own3, far, side, side_b, block0, block1, block2a, block2b, block3 = refs
    rows = own0.shape[1]
    copies = []
    for i, (mine, theirs) in enumerate(
        (
            (own0.at[0], side.at[0]),
            (own1.at[0], side.at[1]),
            (far.at[2], side_b.at[4]),
            (own3.at[0], side.at[2]),
        )
    ):
        start = 2 * rows * i
        copies.append((mine, full.at[pl.ds(start + low * rows, rows), :]))
        copies.append((theirs, full.at[pl.ds(start + (1 - low) * rows, rows), :]))
    for at, size, block in (
        (8, 2, block0),
        (10, 2, block1),
        (12, 1, block2a),
        (13, 1, block2b),
        (14, 2, block3),
    ):
        copies.append((block.at[0], full.at[pl.ds(at * rows, size * rows), :]))
    return copies


def chunk(i, size=WIDE):
    return pl.ds(pl.multiple_of(i * size, size), size)


def row_pieces(refs, first, full):
    copies = []
    for core, (home, seen) in enumerate((refs[:2], refs[2:])):
        for z in range(4):
            at = (core * 8 + z) * MOST
            copies.append((home.at[z, pl.ds(first, MOST)], full.at[pl.ds(at, MOST)]))
            copies.append((seen.at[z], full.at[pl.ds(at + 4 * MOST, MOST)]))
    return copies


def forward_kernel(place, *refs):
    row_refs, pieces, (hid_ref, fa_ref, fb_ref, rows_ref, full, sems, row_sems) = (
        refs[:4],
        refs[4:14],
        refs[14:],
    )
    started = fetch(row_pieces(row_refs, 0, rows_ref), row_sems)
    started += fetch(gate_up_pieces(place[2], pieces, full), sems)
    for copy in started:
        copy.wait()

    def step(i, unused):
        gate = dot(rows_ref[...], full[0, :, chunk(i)], ((1,), (0,)))
        up = dot(rows_ref[...], full[1, :, chunk(i)], ((1,), (0,)))
        sig = 1.0 / (1.0 + jnp.exp(-gate))
        silu = gate * sig
        hid_ref[:, chunk(i)] = (silu * up).astype(BF16)
        fa_ref[:, chunk(i)] = up * sig * (1.0 + gate * (1.0 - sig))
        fb_ref[:, chunk(i)] = silu
        return unused

    lax.fori_loop(0, hid_ref.shape[1] // WIDE, step, 0)


def term_of(at, rows_ref, right_ref):
    return dot(rows_ref[:, at], right_ref[...], ((0,), (0,))).astype(BF16)


def down_term_kernel(place, hid_ref, *refs):
    row_refs, (keep, give, mir0, mir1, mir2, mir3) = refs[:4], refs[4:10]
    rows_ref, terms, row_sems, sems = refs[10:]
    for copy in fetch(row_pieces(row_refs, MOST, rows_ref), row_sems):
        copy.wait()
    low = place[2]
    rows = keep.shape[1]
    half = terms.shape[0] // 2
    owns, mirs = [], []
    for i in range(4):
        start = 2 * rows * i
        owns.append((terms.at[pl.ds(start + low * rows, rows), :], keep.at[i]))
        owns.append((terms.at[pl.ds(start + (1 - low) * rows, rows), :], give.at[i]))
    for i, mir in enumerate((mir0, mir1, mir2, mir3)):
        mirs.append((terms.at[pl.ds(half + 2 * i * rows, 2 * rows), :], mir.at[0]))
    terms[:half, :] = term_of(slice(0, half), rows_ref, hid_ref)
    started = fetch(owns, sems)
    terms[half:, :] = term_of(slice(half, 2 * half), rows_ref, hid_ref)
    started += fetch(mirs, row_sems)
    for copy in started:
        copy.wait()


def gradient_kernel(place, fa_ref, fb_ref, *refs):
    grad_refs, tok_refs, pieces, refs = refs[:4], refs[4:8], refs[8:19], refs[19:]
    both_ref, blk0, blk1, blk2, blk3, keep, give_a, give_b = refs[:8]
    g_rows, x_rows, full, terms, in_sems, out_sems, g_sems, x_sems = refs[8:]
    low = place[2]
    rows = give_b.shape[2]
    started = fetch(row_pieces(grad_refs, MOST, g_rows), g_sems)
    started += fetch(down_pieces(low, pieces, full), in_sems)
    later = fetch(row_pieces(tok_refs, 0, x_rows), x_sems)
    for copy in started:
        copy.wait()

    def step(i, unused):
        hidden_grad = dot(g_rows[...], full[:, chunk(i)], ((1,), (0,)))
        both_ref[0, :, chunk(i)] = (hidden_grad * fa_ref[:, chunk(i)]).astype(BF16)
        both_ref[1, :, chunk(i)] = (hidden_grad * fb_ref[:, chunk(i)]).astype(BF16)
        return unused

    lax.fori_loop(0, both_ref.shape[2] // WIDE, step, 0)
    for copy in later:
        copy.wait()

    half = terms.shape[1] // 2
    blocks, mirs = [], []
    for i, blk in enumerate((blk0, blk1, blk2, blk3)):
        blocks.append((terms.at[:, pl.ds(2 * rows * i, 2 * rows), :], blk))
    for i, give in enumerate((give_b.at[0], give_a.at[1], give_a.at[0], give_b.at[1])):
        start = (8 + 2 * i) * rows
        mirs.append((terms.at[:, pl.ds(start + (1 - low) * rows, rows), :], keep.at[i]))
        mirs.append((terms.at[:, pl.ds(start + low * rows, rows), :], give))
    started = []
    for copies, first, sems in ((blocks, 0, in_sems), (mirs, half, out_sems)):
        at = slice(first, first + half)

        def put(i, unused, at=at):
            terms[i, at, :] = dot(x_rows[:, at], both_ref[i], ((0,), (0,))).astype(BF16)
            return unused

        lax.fori_loop(0, 2, put, 0)
        started += fetch(copies, sems)
    for copy in started:
        copy.wait()


def output_kernel(place, hid_ref, both_ref, *refs):
    up_pieces, dn_pieces, refs = refs[:10], refs[10:21], refs[21:]
    out_mine, grad_mine, theirs, full, down, sems, down_sems = refs
    low = place[2]
    first = fetch(down_pieces(low, dn_pieces, down), down_sems)
    second = fetch(gate_up_pieces(low, up_pieces, full), sems)
    count = out_mine.shape[0]
    for copy in first:
        copy.wait()

    half = down.shape[0] // 2

    def out_step(i, unused):
        at = chunk(i, half)
        out_mine[:, at] = dot(hid_ref[:count, :], down[at, :], ((1,), (1,)))
        theirs[:count, at] = dot(hid_ref[count:, :], down[at, :], ((1,), (1,))).astype(BF16)
        return unused

    lax.fori_loop(0, 2, out_step, 0)
    for copy in second:
        copy.wait()

    def grad_step(i, unused):
        at = chunk(i, half)
        gate, up = full[0, at, :], full[1, at, :]
        for mine, to in ((slice(0, count), grad_mine), (slice(count, 2 * count), theirs)):
            total = dot(both_ref[0, mine, :], gate, ((1,), (1,))) + dot(
                both_ref[1, mine, :], up, ((1,), (1,))
            )
            to[mine if to is theirs else slice(None), at] = total.astype(to.dtype)
        return unused

    lax.fori_loop(0, 2, grad_step, 0)


STEP = 64


def sum_rows(to, *terms):
    def step(i, unused):
        at = chunk(i, STEP)
        to[at, :] = sum(t[at, :].astype(F32) for t in terms).astype(to.dtype)
        return unused

    lax.fori_loop(0, to.shape[0] // STEP, step, 0)


def near_kernel(place, blk_far, blk1, keep, got_a, dn_far, mir3, own_far, own_sum, blk, both):
    rows = both.shape[1]
    for g in range(2):
        sum_rows(blk.at[g], blk_far.at[g], blk1.at[g])
        sum_rows(both.at[g], keep.at[2, g], got_a.at[0, g])
        at = slice(g * rows, (g + 1) * rows)
        sum_rows(both.at[2 + g], dn_far.at[0, at], mir3.at[0, at])
    sum_rows(both.at[4], own_far.at[0], own_sum.at[3])


def widen_kernel(place, keep, got, *outs):
    first = place[3] == 0
    part = keep.shape[2]
    for i, out in enumerate(outs):
        extra = 2 * part - out.shape[2]
        out[0, :, :part] = jnp.where(first, keep[i], got[i]).astype(F32)
        out[0, :, part:] = jnp.where(first, got[i, :, extra:], keep[i, :, extra:]).astype(F32)


def run(kernel, name, place, local, remote, outs, far_outs, scratch, flops):
    vmem, anywhere = pl.BlockSpec(memory_space=pltpu.VMEM), pl.BlockSpec(memory_space=pl.ANY)
    shapes = [jax.ShapeDtypeStruct(*o) for o in tuple(outs) + tuple(far_outs)]
    size = sum(a.size * a.dtype.itemsize for a in (*local, *remote))
    size += sum(a.size * a.dtype.itemsize for a in shapes)
    return pl.pallas_call(
        kernel,
        out_shape=shapes,
        in_specs=[pl.BlockSpec(memory_space=pltpu.SMEM)]
        + [vmem] * len(local)
        + [anywhere] * len(remote),
        out_specs=[vmem] * len(outs) + [anywhere] * len(far_outs),
        scratch_shapes=scratch,
        compiler_params=pltpu.CompilerParams(vmem_limit_bytes=44 << 20),
        cost_estimate=pl.CostEstimate(
            flops=flops, bytes_accessed=size, transcendentals=0
        ),
        name=name,
    )(place, *local, *remote)


def on_device(tokens, expert_ids, gate_vals, w_gate, w_up, w_down, cotangent):
    core = lax.axis_index("expert") % 2
    y, x = lax.axis_index("fsdp") // 4, lax.axis_index("fsdp") % 4
    side, low = x // 2, x % 2
    rows, width = w_gate.shape[1:]
    depth = tokens.shape[1]
    part = half_width(width)
    quarter = 4 * MOST
    count = 4 * quarter
    work = count * depth * part * 2
    dma, row_dma = pltpu.SemaphoreType.DMA((13,)), pltpu.SemaphoreType.DMA((16,))
    row_scratch = pltpu.VMEM((count, depth), BF16)
    place = jnp.stack([y, side, low, core]).astype(jnp.int32)
    ids, gates = expert_ids.T, gate_vals.T
    r = Rounds()
    send = r.send

    def join(*arrays):
        return jnp.concatenate(arrays, axis=0)

    slices = ((3, rows, part), BF16)
    keep, give = run(
        split_kernel,
        "split",
        place,
        (),
        (w_gate, w_up, w_down),
        [slices] * 2,
        [],
        [pltpu.VMEM((3, rows, width), BF16), pltpu.SemaphoreType.DMA((3,))],
        1,
    )
    got = send("core", give)
    own_gu, own_dn, away_gu, away_dn = run(
        choose_kernel,
        "choose",
        place,
        (keep, got),
        (),
        [((2, rows, part), BF16), ((1, rows, part), BF16)] * 2,
        [],
        [],
        1,
    )
    r.next()
    side_gu = send("side", own_gu)
    mir0 = send("mirror", away_gu)
    own3 = send("up", own_dn)
    own1 = send("down", own_dn)
    r.next()
    block0 = in_pair(low == 0, own_gu, side_gu, 1)
    mir3 = send("up", mir0)
    mir1 = send("down", mir0)
    dn_mir = send("mirror", away_dn)
    both, oth, goth = dispatch(r.late(place), ids, gates, tokens, cotangent)
    home = r.exchange(r.late(both).reshape(4, 2 * MOST, depth), 2)
    r.next()
    block3 = send("up", block0)
    far = send("down", join(mir1, own1))
    side_a = send("side", join(mir0, mir1, dn_mir))
    tok_mir = send("mirror", oth)
    r.next()
    block_dn = in_pair(low == 1, dn_mir, side_a[4:], 1)
    block2 = send("up", block3)
    block1 = send("down", block0)
    side_b = send("side", join(mir3, far))
    grad_mir = send("mirror", goth)
    home_got = r.hold(lax.ppermute(r.late(home), AXES, TO_CORE))
    seen_tok = r.exchange(tok_mir.reshape(4, MOST, depth), 2)
    r.next()
    dn3 = send("up", block_dn)
    dn1 = send("down", block_dn)
    own_side = send("side", join(own_dn, own1, own3))
    tok_got = r.hold(lax.ppermute(after(seen_tok, side_b), AXES, TO_CORE))
    token_rows = (home, seen_tok, home_got, tok_got)
    gu_pieces = (block0, block1, block2, block3, mir0, mir1, mir3, far, side_a, side_b)
    hidden, fa, fb = run(
        forward_kernel,
        "forward",
        r.late(place),
        (),
        token_rows + gu_pieces,
        [((count, part), BF16), ((count, part), F32), ((count, part), F32)],
        [],
        [row_scratch, pltpu.VMEM((2, depth, part), BF16), dma, row_dma],
        2 * work,
    )
    r.hold(hidden)
    seen_grad = r.exchange(r.late(grad_mir).reshape(4, MOST, depth))
    r.next()
    dn2a = send("up", r.pin(dn3)[:, :rows])
    dn2b = send("down", r.pin(dn1)[:, rows:])
    grad_got = r.hold(lax.ppermute(r.pin(seen_grad), AXES, TO_CORE))
    grad_rows = (home, seen_grad, home_got, grad_got)
    own_keep, own_give, mir_t0, mir_t1, mir_t2, mir_t3 = run(
        down_term_kernel,
        "down_term",
        place,
        (r.pin(hidden),),
        grad_rows,
        [],
        [((4, rows, part), BF16)] * 2 + [((1, 2 * rows, part), BF16)] * 4,
        [row_scratch, pltpu.VMEM((depth, part), BF16), row_dma, dma],
        work,
    )
    r.hold(own_give)
    r.next()
    dn_pieces = (own_dn, own1, own3, far, own_side, side_b, block_dn, dn1, dn2a, dn2b, dn3)
    dn_far = send("down", mir_t2)
    dn_back = send("up", mir_t1)
    own_got = send("side", own_give)
    hidden_grads, blk_t0, blk_t1, blk_t2, blk_t3, mir_keep, give_a, give_b = run(
        gradient_kernel,
        "gradient",
        place,
        (r.pin(fa), fb),
        grad_rows + token_rows + dn_pieces,
        [((2, count, part), BF16)],
        [((2, 2 * rows, part), BF16)] * 4
        + [((4, 2, rows, part), BF16)]
        + [((2, 2, rows, part), BF16)] * 2,
        [row_scratch, row_scratch]
        + [pltpu.VMEM((depth, part), BF16), pltpu.VMEM((2, depth, part), BF16)]
        + [dma, dma, row_dma, row_dma],
        3 * work,
    )
    r.hold(give_a)

    r.next()
    own_sum = add(own_keep, own_got)
    blk_far = send("up", blk_t2)
    blk_back = send("down", blk_t3)
    got_a = send("side", give_a)
    own_far = send("down", own_sum[2:3])
    out_mine, grad_mine, theirs = run(
        output_kernel,
        "outputs",
        place,
        (r.pin(hidden), hidden_grads),
        gu_pieces + dn_pieces,
        [((count // 2, depth), F32)] * 2 + [((count, depth), BF16)],
        [],
        [pltpu.VMEM((2, depth, part), BF16), pltpu.VMEM((depth, part), BF16), dma, dma],
        3 * work,
    )
    r.hold(theirs)
    r.next()
    blk_mid, both_mid = run(
        near_kernel,
        "near",
        place,
        (r.pin(blk_far), blk_t1, mir_keep, got_a, dn_far, mir_t3, own_far, own_sum),
        (),
        [((2, 2 * rows, part), BF16), ((5, rows, part), BF16)],
        [],
        [],
        1,
    )
    blk_near = send("up", blk_mid)
    got_b = send("side", give_b)
    both_far = send("down", both_mid)
    got = send("core", theirs)
    out = r.hold(add(r.late(out_mine), got[: 2 * quarter]))
    out_home = r.exchange(out[quarter:].reshape(4, MOST, depth))
    grd = r.hold(add(r.late(grad_mine), got[2 * quarter :]))
    grad_home = r.exchange(grd[quarter:].reshape(4, MOST, depth), 2)
    r.next()
    both_far, blk_near, blk_back = r.pin(both_far), r.pin(blk_near), r.pin(blk_back)
    mir_far, own_near = both_far[:2], both_far[4:]
    dn_near = both_far[2:4].reshape(1, 2 * rows, part)
    mir_back = send("up", jnp.concatenate([add(mir_keep[1], got_a[1]), own_sum[1:2]], axis=0))
    mir_near = send("down", add(mir_far, mir_keep[3], r.pin(got_b)[1]))
    blk = add(blk_t0, blk_back, blk_near)
    mir_dn = add(mir_t0, dn_back, dn_near)
    low_half, high_half = join(blk[:, :rows], mir_dn[:, rows:]), join(blk[:, rows:], mir_dn[:, :rows])
    stay = jnp.where(low == 0, low_half, high_half)
    leave_got = send("side", jnp.where(low == 0, high_half, low_half))
    out_oth = send("mirror", out_home.reshape(quarter, depth))
    own_rows = r.hold(
        jnp.concatenate(
            [r.late(v[:quarter]).reshape(4, MOST, depth) for v in (out, grd)], axis=1
        )
    )
    r.next()
    here = core == side
    mir_back = r.pin(mir_back)
    mine = add(stay, r.pin(leave_got))
    gu_mir = add(mir_keep[0], got_b[0], mir_back[:2], r.pin(mir_near))
    away = send("mirror", join(gu_mir, mine[2:]))
    grad_oth = send("mirror", grad_home.reshape(quarter, depth))
    owned = r.exchange(own_rows)
    out_own = owned[:, :MOST].reshape(quarter, depth)
    grad_own = owned[:, MOST:].reshape(quarter, depth)
    own = join(mine[:2], add(own_sum[:1], mir_back[2:], own_near))
    other = lax.ppermute(jnp.where(here, away, own), AXES, TO_CORE)
    kept = jnp.where(here, own, away)
    wide = ((1, rows, width), F32)
    grad_gate, grad_up, grad_down = run(
        widen_kernel, "widen", place, (kept, other), (), [wide] * 3, [], [], 1
    )

    output, grad_tokens, grad_gates = combine(
        after(place, grad_down), ids, gates, cotangent, out_own, out_oth, grad_own, grad_oth
    )
    return (output, grad_tokens, grad_gates.T, grad_gate, grad_up, grad_down)


def solution(mesh):
    rows, weight = P(AXES, None), P("expert", "fsdp", None)
    return jax.shard_map(
        on_device,
        mesh=mesh,
        in_specs=(rows, rows, rows, weight, weight, weight, rows),
        out_specs=(rows, rows, rows, weight, weight, weight),
        check_vma=False,
    )
```
